128 devices in a mesh: dp: 32 (over z, x, core), mp: 4 (over y).
Axes of the slice: x: 4, y: 4, z: 4, core: 2. Of those that a mesh axis runs over, the one named last changes fastest.
Arguments:
- feat_values: bfloat16 [262144, 8, 128], P('dp', 'mp'), may hold values from -6 to 6
- feat_blocks: int32 [262144, 8], P('dp', 'mp'), may hold values from 0 to 127
- fixed_coef: float32 [128, 128], replicated, may hold values from -0.1875 to 0.1875
- member_of: int32 [262144, 1], P(('dp', 'mp')), may hold values from 0 to 511; in each aligned block of 2048 rows (0 to 2047, 2048 to 4095, ...) at most 8 rows name the same one
- labels: int32 [262144], P(('dp', 'mp')), may hold values 0 or 1
- re_features: bfloat16 [262144, 256], P(('dp', 'mp')), may hold values from -6.5 to 6.5
- member_slot: int32 [512], replicated, may hold values from 0 to 511, each once
- coef: float32 [512, 256], P(('dp', 'mp')), may hold values from -0.9 to 0.9
Outputs:
- new_coef: float32 [512, 256], P(('dp', 'mp'))
- member_objective: float32 [512], P(('dp', 'mp'))
- new_margin: float32 [262144], P(('dp', 'mp'))
The draws below stay inside these ranges and needn't reach their ends.
Inputs may be any that keep to these rules, and one draw needn't show every extreme that they name: `member_of`: among the rows of one device (aligned blocks of 2048 impressions) no member appears more than 8 times, and some member appears exactly 8 times in some blocks; every member appears somewhere. `member_slot` is a permutation; coefficient row m (the member whose member_slot is m) lives on device m // 4 of dp+mp.
All inputs are finite; a program needn't handle non-finite values. No bound on the sum of `labels` on one device may be relied on, other than what follows from the above.
Results may differ from the reference program's by a relative error of at most 0.0089.
Values may be sent and summed in bfloat16 or wider, within the bound.
A program may use at most 128 MiB of HBM per device.

```python
import math
import jax
import jax.numpy as jnp
import numpy as np
from jax import lax

R = 256
FB = 128
NBLK = 128
NNZB = 8
CAP = 8
ROW_DEV = 2048
ROWS = 262144
MEMBERS = 512
N_DP = 32
N_MP = 4


def draw_re_features(key, part):
    entries = jax.random.truncated_normal(key, -3.0, 3.0, (ROWS, R + 3), jnp.float32)
    row_scale = jnp.ones((ROWS, 1), jnp.float32)
    summed = entries[:, 0:R] + entries[:, 1:R + 1] + entries[:, 2:R + 2] + entries[:, 3:R + 3]
    return (0.45 * row_scale * summed).astype(jnp.bfloat16)


def plant(result, key, low, top_value):
    longest = result.shape.index(max(result.shape))
    spots = []
    for shift in (0, 1):
        where = [jax.random.randint(jax.random.fold_in(key, axis), (), 0, length) for axis, length in enumerate(result.shape)]
        where[longest] = (where[longest] + shift) % result.shape[longest]
        spots.append(tuple(where))
    return result.at[spots[0]].set(low).at[spots[1]].set(top_value)


def levels(stream_key, shape, cuts, low, top_value):
    def one(position, parts):
        draws = jax.random.uniform(jax.random.fold_in(jax.random.fold_in(stream_key, 6), position), (parts,), jnp.float32, low / len(cuts), top_value / len(cuts))
        return jnp.repeat(jnp.exp(draws), shape[position] // parts).reshape((-1,) + (1,) * (len(shape) - position - 1))

    factor_of = one(*cuts[0])
    for cut in cuts[1:]:
        factor_of = factor_of * one(*cut)
    return factor_of


def routed_block(stream_key, own, number, rows, number_of, top, bound, skew):
    ranking = jax.random.permutation(stream_key, number_of)
    packed, ordinary = load_shares(number_of, rows * top, bound, skew, True), load_shares(number_of, rows * top, bound, skew, False)
    places = jnp.arange(number_of)

    def named(lengths, turn):
        used = int((lengths > 0).sum())
        fixed = max(1, used // 4)
        passed = fixed + (places - fixed + turn * (used - fixed)) % max(1, number_of - fixed)
        return jnp.zeros((number_of,), jnp.int32).at[ranking[jnp.where(places < fixed, places, passed)]].set(jnp.asarray(lengths, jnp.int32))

    lengths = jnp.where(number % 4 == 0, named(packed, number // 4), named(ordinary, number - number // 4 - 1))
    mixed = jax.random.permutation(jax.random.fold_in(own, 3), number_of)
    giver, sink = mixed[0:number_of // 2 * 2:2], mixed[1:number_of // 2 * 2:2]
    slack = jnp.minimum(lengths[giver] - 1, bound - lengths[sink]) // 2
    slack = jnp.where((giver == ranking[0]) | (sink == ranking[0]) | (lengths[sink] == 0), 0, jnp.maximum(slack, 0))
    passed = jax.random.randint(jax.random.fold_in(own, 4), (number_of // 2,), 0, 1 << 20) % (slack + 1)
    lengths = lengths.at[giver].add(-passed).at[sink].add(passed)
    items = jnp.searchsorted(jnp.cumsum(lengths), jnp.arange(rows * top), side="right").astype(jnp.int32)
    listing = items.reshape(top, rows).T
    listing = listing[jax.random.permutation(jax.random.fold_in(own, 1), rows)]
    turn = jax.random.randint(jax.random.fold_in(own, 2), (rows, 1), 0, top)
    return jnp.take_along_axis(listing, (jnp.arange(top)[None, :] + turn) % top, axis=1)


def load_shares(count, total, reach, slope, full):
    weights = [(1 << 20) // math.isqrt(standing ** slope) + 1 for standing in range(1, count + 1)]
    largest = reach if full else min(reach, max(-(-total // count), total * weights[0] // sum(weights)))
    least = 1 if total - largest >= count - 1 else 0
    given, surplus = [largest] + [least] * (count - 1), total - largest - least * (count - 1)
    while surplus > 0:
        free = [i for i in range(1, count) if given[i] < largest] or [i for i in range(1, count) if given[i] < reach]
        pool, left = sum([weights[i] for i in free]), surplus
        for i in free:
            more = min(reach - given[i], max(1, left * weights[i] // pool), surplus)
            given[i] = given[i] + more
            surplus = surplus - more
    return np.array(given)


def noise(stream_key, extent, deviation, most, cuts=(), held_as=jnp.bfloat16):
    loudness = levels(stream_key, extent, cuts, -0.22, 0.18) if cuts else 1.0
    values = jax.random.normal(stream_key, extent, jnp.float32) * deviation * loudness
    return jnp.minimum(jnp.maximum(values, -most), most).astype(held_as)


def setup_inputs(seed: int = 0) -> dict:
    arg_keys = jax.random.split(jax.random.key(seed), 9)
    feat_values = noise(arg_keys[0], (ROWS, NNZB, FB), 1.0, 6.0, ((0, 32), (1, 4)))
    feat_blocks = plant(jax.random.randint(arg_keys[1], (ROWS, NNZB), 0, NBLK), jax.random.fold_in(arg_keys[1], 1), 0, NBLK - 1).astype(jnp.int32)
    fixed_coef = noise(arg_keys[2], (NBLK, FB), (NNZB * FB) ** -0.5, 0.1875, (), jnp.float32)
    member_of_keys = jax.random.split(jax.random.fold_in(arg_keys[3], 1), ROWS // ROW_DEV)
    member_of_turns = jax.random.permutation(jax.random.fold_in(arg_keys[3], 3), ROWS // ROW_DEV)
    member_of = jax.vmap(lambda own, number: routed_block(jax.random.fold_in(arg_keys[3], 2), own, number, ROW_DEV, MEMBERS, 1, CAP, 2))(member_of_keys, member_of_turns).reshape((ROWS, 1))
    labels = plant((jax.random.randint(arg_keys[4], (ROWS,), 0, 2) < 1).astype(jnp.int32), jax.random.fold_in(arg_keys[4], 1), 0, 1)
    re_features = draw_re_features(jax.random.fold_in(arg_keys[8], 71), 0)
    member_slot = jax.random.permutation(arg_keys[6], MEMBERS).astype(jnp.int32)
    coef = noise(arg_keys[7], (MEMBERS, R), 0.15, 0.9, ((0, 128),), jnp.float32)
    return {"feat_values": feat_values, "feat_blocks": feat_blocks, "fixed_coef": fixed_coef, "member_of": member_of, "labels": labels, "re_features": re_features, "member_slot": member_slot, "coef": coef}


LAMBDA = 1.0

def member_terms(rows_z, rows_fixed, rows_label, live, coef_row):
    hi = lax.Precision.HIGHEST
    zfull = rows_z.astype(jnp.float32)
    coef_b = coef_row.astype(jnp.bfloat16).astype(jnp.float32)
    score = rows_fixed + jnp.dot(zfull, coef_b, precision=hi)
    probability = jax.nn.sigmoid(score)
    weight = live * probability * (1.0 - probability)
    residual = (live * (rows_label - probability)).astype(jnp.bfloat16).astype(jnp.float32)
    weighted = (weight[:, None] * zfull).astype(jnp.bfloat16).astype(jnp.float32)
    hessian = jnp.dot(weighted.T, zfull, precision=hi) + LAMBDA * jnp.eye(R, dtype=jnp.float32)
    gradient = jnp.dot(residual, zfull, precision=hi) - LAMBDA * coef_row
    factor = jnp.linalg.cholesky(hessian)
    update = jax.scipy.linalg.cho_solve((factor, True), gradient)
    logdet = 2.0 * jnp.sum(jnp.log(jnp.diagonal(factor)))
    loglik = jnp.sum(live * (rows_label * score - jax.nn.softplus(score)))
    objective = loglik - 0.5 * LAMBDA * jnp.sum(coef_row * coef_row) - 0.5 * logdet
    return (coef_row + update, objective)

def reference(feat_values, feat_blocks, fixed_coef, member_of, labels, re_features, member_slot, coef):
    devices = N_DP * N_MP
    rows = re_features.shape[0]
    members = member_slot.shape[0]
    padded = CAP * devices

    def fixed_block(pair):
        values, blocks = pair
        return jnp.sum(values.astype(jnp.float32) * fixed_coef[blocks], axis=(1, 2))
    fixed = lax.map(fixed_block, (feat_values.reshape(devices, ROW_DEV, NNZB, FB), feat_blocks.reshape(devices, ROW_DEV, NNZB))).reshape(rows)
    member = member_of[:, 0]
    order = jnp.argsort(member, stable=True)
    counts = jnp.zeros((members,), jnp.int32).at[member].add(1)
    starts = (jnp.cumsum(counts) - counts).astype(jnp.int32)
    sorted_z = jnp.concatenate([re_features[order], jnp.zeros((padded, R), jnp.bfloat16)], 0)
    sorted_fixed = jnp.concatenate([fixed[order], jnp.zeros((padded,), jnp.float32)])
    sorted_label = jnp.concatenate([labels[order].astype(jnp.float32), jnp.zeros((padded,), jnp.float32)])
    member_at = jnp.zeros((members,), jnp.int32).at[member_slot].set(jnp.arange(members, dtype=jnp.int32))

    def solve_member(slot):
        member_id = member_at[slot]
        start = starts[member_id].astype(jnp.int32)
        rows_z = lax.dynamic_slice_in_dim(sorted_z, start, padded, 0)
        rows_fixed = lax.dynamic_slice_in_dim(sorted_fixed, start, padded, 0)
        rows_label = lax.dynamic_slice_in_dim(sorted_label, start, padded, 0)
        live = (jnp.arange(padded, dtype=jnp.int32) < counts[member_id]).astype(jnp.float32)
        return member_terms(rows_z, rows_fixed, rows_label, live, coef[slot])
    new_coef, objective = lax.map(solve_member, jnp.arange(members, dtype=jnp.int32))
    new_b = new_coef.astype(jnp.bfloat16)
    slot_of_row = member_slot[member]

    def margin_block(pair):
        features, slots = pair
        return jnp.sum(features.astype(jnp.float32) * new_b[slots].astype(jnp.float32), axis=1)
    random_part = lax.map(margin_block, (re_features.reshape(devices, ROW_DEV, R), slot_of_row.reshape(devices, ROW_DEV))).reshape(rows)
    return (new_coef, objective, fixed + random_part)
```

```python
import functools

import jax
import jax.numpy as jnp
from jax import lax
from jax.experimental import pallas as pl
from jax.experimental.pallas import tpu as pltpu
from jax.sharding import PartitionSpec as P

R = 256
CAP = 8
LAMBDA = 1.0

MESH = pl.DeviceIdType.MESH
F32 = jnp.float32
BF16 = jnp.bfloat16
NT = (((1,), (1,)), ((), ()))
TN = (((0,), (0,)), ((), ()))
MIB = 1 << 20


def iota(shape, axis):
    return lax.broadcasted_iota(jnp.int32, shape, axis)


def halves(x):
    high = x.astype(BF16)
    return high, (x - high.astype(F32)).astype(BF16)


def thirds(x):
    high, rest = x.astype(BF16), None
    rest = x - high.astype(F32)
    middle = rest.astype(BF16)
    return high, middle, (rest - middle.astype(F32)).astype(BF16)


def place(device):
    return (device // 4, lax.rem(device, 4))


def position():
    return lax.axis_index("dp") * 4 + lax.axis_index("mp")


def one_hot(condition):
    return jnp.where(condition, 1.0, 0.0).astype(BF16)


def ring_peers(me):
    inner, outer = lax.rem(me, 8), me // 8
    first = [outer * 8 + lax.rem(inner + k, 8) for k in range(1, 8)]
    x, z = lax.rem(outer, 4), outer // 4
    second = [(z * 4 + lax.rem(x + k, 4)) * 8 + inner for k in range(1, 4)]
    third = [(lax.rem(z + k, 4) * 4 + x) * 8 + inner for k in range(1, 4)]
    return first, second, third


def gather_stage(table, me, stage, send_sem, recv_sem):
    peers = ring_peers(me)[stage]
    rows = (8, 64, 256)[stage]
    block = pl.ds(pl.multiple_of((me * 8) // rows * rows, rows), rows)
    for peer in peers:
        pltpu.make_async_remote_copy(
            src_ref=table.at[block],
            dst_ref=table.at[block],
            send_sem=send_sem.at[stage],
            recv_sem=recv_sem.at[stage],
            device_id=place(peer),
            device_id_type=MESH,
        ).start()

    def finish():
        whole = table.at[pl.ds(0, rows * len(peers))]
        waiting = pltpu.make_async_remote_copy(
            src_ref=whole,
            dst_ref=whole,
            send_sem=send_sem.at[stage],
            recv_sem=recv_sem.at[stage],
            device_id=place(peers[0]),
            device_id_type=MESH,
        )
        waiting.wait_send()
        waiting.wait_recv()

    return finish


def row_products(table, z_ref, slot_ref, out_ref):
    half = [table[pl.ds(h, 512, stride=2), :].astype(BF16) for h in range(2)]
    coefs = jnp.concatenate(half, axis=1)
    for c in range(8):
        lanes = pl.ds(256 * c, 256)
        product = lax.dot_general(coefs, z_ref[lanes, :], NT, preferred_element_type=F32)
        chosen = iota((512, 256), 0) == slot_ref[:, lanes]
        out_ref[:, lanes] = jnp.sum(jnp.where(chosen, product, 0.0), axis=0, keepdims=True)


def dispatch_kernel(
    v_ref, ids_ref, w_ref, member_ref, label_ref, z_ref, slots_ref, coef_ref,
    hess_ref, grad_ref, side_sum_ref, slot_ref, fixed_ref,
    onehot, ids2, part, fixed_part, fixed_recv, table, target_ref, score_ref,
    send, recv, side_send, side_recv,
    send_sem, recv_sem, table_send_sem, table_recv_sem,
):
    me = position()
    mine = lax.axis_index("mp")

    barrier = pltpu.get_barrier_semaphore()

    def greet(k, carry):
        peer = lax.rem(me + k, 128)
        pl.semaphore_signal(barrier, inc=1, device_id=place(peer), device_id_type=MESH)
        return carry

    lax.fori_loop(1, 128, greet, 0)
    table[pl.ds(pl.multiple_of(me * 8, 8), 8), :] = coef_ref[...]

    for c in range(8):
        lanes = pl.ds(256 * c, 256)
        onehot[:, lanes] = one_hot(iota((512, 256), 0) == member_ref[:, lanes])
    slots = slots_ref[...]
    sub = iota((8, 512), 0)
    owner_row = jnp.where(sub == 0, slots // 4, jnp.where(sub == 1, lax.rem(slots, 4), 0))
    owner_row = owner_row.astype(F32).astype(BF16)
    before = one_hot(iota((256, 256), 0) < iota((256, 256), 1))
    tally = jnp.concatenate([before, jnp.ones((256, 256), BF16)], axis=1)
    base = jnp.zeros((512, 256), F32)
    for c in range(8):
        lanes = pl.ds(256 * c, 256)
        hot = onehot[:, lanes]
        found = jnp.dot(owner_row, hot, preferred_element_type=F32)
        counted = jnp.dot(hot, tally, preferred_element_type=F32)
        rank = jnp.sum(hot.astype(F32) * (base + counted[:, :256]), axis=0, keepdims=True)
        base = base + counted[:, 256:]
        slot = found[0:1] * 4.0 + found[1:2]
        slot_ref[:, lanes] = slot.astype(jnp.int32)
        target_ref[:, lanes] = (slot * 8.0 + rank).astype(jnp.int32)

    pl.semaphore_wait(barrier, 127)
    finish_first = gather_stage(table, me, 0, table_send_sem, table_recv_sem)

    for r in range(64):
        for k in range(2):
            ids2[k, r:r + 1, :] = ids_ref[k:k + 1, 128 * r:128 * r + 128]
    spread = [one_hot(iota((128, 256), 1) == 2 * iota((128, 256), 0) + k) for k in range(2)]
    ids = sum(
        jnp.dot(ids2[k].astype(F32).astype(BF16), spread[k], preferred_element_type=F32)
        for k in range(2)
    )
    part[...] = ids
    w2 = jnp.concatenate(halves(w_ref[...]), axis=1)

    def margin_rows(r, carry):
        rows = v_ref[pl.ds(pl.multiple_of(r * 256, 256), 256), :]
        product = lax.dot_general(
            w2, jnp.concatenate([rows, rows], axis=1), NT, preferred_element_type=F32
        )
        chosen = iota((128, 256), 0) == part[pl.ds(r, 1), :].astype(jnp.int32)
        part[pl.ds(r, 1), :] = jnp.sum(jnp.where(chosen, product, 0.0), axis=0, keepdims=True)
        return carry

    lax.fori_loop(0, 64, margin_rows, 0, unroll=4)
    pairs = one_hot(iota((256, 128), 0) // 2 == iota((256, 128), 1))
    fixed_part[...] = sum(
        jnp.dot(piece, pairs, preferred_element_type=F32) for piece in thirds(part[...])
    )
    for k in range(1, 4):
        other = lax.rem(mine + k, 4)
        pltpu.make_async_remote_copy(
            src_ref=fixed_part.at[pl.ds(pl.multiple_of(other * 16, 16), 16)],
            dst_ref=fixed_recv.at[pl.ds(k * 16, 16)],
            send_sem=send_sem.at[0],
            recv_sem=recv_sem.at[0],
            device_id=(lax.axis_index("dp"), other),
            device_id_type=MESH,
        ).start()

    finish_first()
    finish_second = gather_stage(table, me, 1, table_send_sem, table_recv_sem)

    waiting = pltpu.make_async_remote_copy(
        src_ref=fixed_part.at[pl.ds(0, 48)],
        dst_ref=fixed_recv.at[pl.ds(16, 48)],
        send_sem=send_sem.at[0],
        recv_sem=recv_sem.at[0],
        device_id=(lax.axis_index("dp"), mine),
        device_id_type=MESH,
    )
    waiting.wait_send()
    waiting.wait_recv()
    own = fixed_part[pl.ds(pl.multiple_of(mine * 16, 16), 16), :]
    total = own + fixed_recv[16:32] + fixed_recv[32:48] + fixed_recv[48:64]
    for r in range(16):
        fixed_ref[:, 128 * r:128 * r + 128] = total[r:r + 1, :]

    finish_second()
    finish_third = gather_stage(table, me, 2, table_send_sem, table_recv_sem)

    def send_rows(c, carry):
        chunk = lax.rem(me // 8 + c, 16)
        target = target_ref[...] - chunk * 256
        picked = jnp.zeros((256, 256), F32)
        for piece in range(4):
            lanes = pl.ds(512 * piece, 512)
            hot = one_hot(iota((256, 512), 0) == target[:, 512 * piece:512 * piece + 512])
            picked = picked + jnp.dot(hot, z_ref[lanes, :], preferred_element_type=F32)
        send[pl.ds(chunk * 8, 8)] = picked.astype(BF16).reshape(8, 32, 256)

        def send_one(j, inner):
            owner = chunk * 8 + lax.rem(me + j, 8)

            @pl.when(owner != me)
            def _():
                pltpu.make_async_remote_copy(
                    src_ref=send.at[owner],
                    dst_ref=recv.at[me],
                    send_sem=send_sem.at[1],
                    recv_sem=recv_sem.at[1],
                    device_id=place(owner),
                    device_id_type=MESH,
                ).start()

            return inner

        return lax.fori_loop(0, 8, send_one, carry)

    lax.fori_loop(0, 16, send_rows, 0)
    recv[pl.ds(me, 1)] = send[pl.ds(me, 1)]

    finish_third()
    row_products(table, z_ref, slot_ref, score_ref)
    score = score_ref[...] + fixed_ref[...]
    label = label_ref[...].astype(F32)
    small = jnp.exp(-jnp.abs(score))
    probability = jnp.where(score >= 0.0, 1.0, small) / (1.0 + small)
    weight = small / ((1.0 + small) * (1.0 + small))
    residual = label - probability
    likelihood = label * score - (jnp.maximum(score, 0.0) + jnp.log1p(small))
    target = target_ref[...]
    total_side = jnp.zeros((128, 128), F32)
    for c in range(4):
        lanes = slice(512 * c, 512 * c + 512)
        owner_hot = one_hot(iota((128, 512), 0) == target[:, lanes] // 32)
        within = iota((32, 512), 0) == lax.rem(target[:, lanes], 32)
        sides = jnp.concatenate(
            [jnp.where(within, q[:, lanes], 0.0) for q in (weight, residual, likelihood)]
            + [jnp.zeros((32, 512), F32)],
            axis=0,
        )
        for piece in halves(sides):
            total_side = total_side + lax.dot_general(
                owner_hot, piece, NT, preferred_element_type=F32
            )
    for d in range(128):
        side_send[d] = total_side[d:d + 1, :]

    def send_side(k, carry):
        owner = lax.rem(me + k, 128)
        pltpu.make_async_remote_copy(
            src_ref=side_send.at[owner],
            dst_ref=side_recv.at[me],
            send_sem=send_sem.at[2],
            recv_sem=recv_sem.at[2],
            device_id=place(owner),
            device_id_type=MESH,
        ).start()
        return carry

    lax.fori_loop(1, 128, send_side, 0)
    side_recv[pl.ds(me, 1)] = side_send[pl.ds(me, 1)]

    for number, sent, got in ((1, send, recv), (2, side_send, side_recv)):
        waiting = pltpu.make_async_remote_copy(
            src_ref=sent.at[pl.ds(0, 127)],
            dst_ref=got.at[pl.ds(0, 127)],
            send_sem=send_sem.at[number],
            recv_sem=recv_sem.at[number],
            device_id=place(me),
            device_id_type=MESH,
        )
        waiting.wait_send()
        waiting.wait_recv()

    side_sum_ref[...] = jnp.sum(side_recv[...], axis=0)
    eye = jnp.where(iota((256, 256), 0) == iota((256, 256), 1), LAMBDA, 0.0)
    for m in range(4):
        hess_ref[m] = eye
    grad_ref[...] = jnp.zeros((4, 8, 256), F32)
    ones = jnp.ones((256, 128), BF16)

    def accumulate(c, carry):
        sources = pl.ds(pl.multiple_of(c * 32, 32), 32)
        sides = jnp.broadcast_to(side_recv[sources], (32, 8, 128))
        lane = iota((32, 8, 128), 2) - iota((32, 8, 128), 1)
        for m in range(4):
            rows = recv[sources, 8 * m:8 * m + 8, :].astype(F32).reshape(256, 256)
            rows_b = rows.astype(BF16)
            column = []
            for quantity in range(2):
                chosen = lane == 32 * quantity + 8 * m
                picked = jnp.where(chosen, sides, 0.0).reshape(256, 128)
                picked = jnp.concatenate(halves(picked), axis=1)
                column.append(jnp.dot(picked, ones, preferred_element_type=F32))
            weights = jnp.concatenate([column[0], column[0]], axis=1)
            weighted = (weights * rows).astype(BF16)
            hess_ref[m] += lax.dot_general(weighted, rows_b, TN, preferred_element_type=F32)
            pull = lax.dot_general(
                column[1].astype(BF16), rows_b, TN, preferred_element_type=F32
            )
            grad_ref[m] += pull[0:8]
        return carry

    lax.fori_loop(0, 4, accumulate, 0)


def dispatch(v, ids, fixed_coef, member, labels, z, slots, coef8):
    vmem = pl.BlockSpec(memory_space=pltpu.VMEM)
    return pl.pallas_call(
        dispatch_kernel,
        out_shape=(
            jax.ShapeDtypeStruct((4, 256, 256), F32),
            jax.ShapeDtypeStruct((4, 8, 256), F32),
            jax.ShapeDtypeStruct((1, 128), F32),
            jax.ShapeDtypeStruct((1, 2048), jnp.int32),
            jax.ShapeDtypeStruct((1, 2048), F32),
        ),
        in_specs=[vmem] * 8,
        out_specs=(vmem,) * 5,
        scratch_shapes=[
            pltpu.VMEM((512, 2048), BF16),
            pltpu.VMEM((2, 64, 128), jnp.int32),
            pltpu.VMEM((64, 256), F32),
            pltpu.VMEM((64, 128), F32),
            pltpu.VMEM((64, 128), F32),
            pltpu.VMEM((1024, 128), F32),
            pltpu.VMEM((1, 2048), jnp.int32),
            pltpu.VMEM((1, 2048), F32),
            pltpu.VMEM((128, 32, 256), BF16),
            pltpu.VMEM((128, 32, 256), BF16),
            pltpu.VMEM((128, 1, 128), F32),
            pltpu.VMEM((128, 1, 128), F32),
            pltpu.SemaphoreType.DMA((3,)),
            pltpu.SemaphoreType.DMA((3,)),
            pltpu.SemaphoreType.DMA((3,)),
            pltpu.SemaphoreType.DMA((3,)),
        ],
        compiler_params=pltpu.CompilerParams(
            collective_id=0, has_side_effects=True, vmem_limit_bytes=48 * MIB
        ),
        name="dispatch",
    )(v, ids, fixed_coef, member, labels, z, slots, coef8)


def dot6(left, right, dims):
    lh, lm, ll = thirds(left)
    rh, rm, rl = thirds(right)
    ((la,), (ra,)), _ = dims
    return lax.dot_general(
        jnp.concatenate([lh, lh, lm, lm, lh, ll], axis=la),
        jnp.concatenate([rh, rm, rh, rm, rl, rh], axis=ra),
        dims,
        preferred_element_type=F32,
    )


def invert_packed(packed, pivots, first):
    lane = iota((32, 128), 1)
    group = lane // 32 * 32
    local = lane - group
    sub = iota((32, 128), 0)
    for j in range(32):
        column = jnp.take_along_axis(packed, group + j, axis=1, mode="promise_in_bounds")
        row = jnp.broadcast_to(packed[j:j + 1], (32, 128))
        pivot = jnp.broadcast_to(column[j:j + 1], (32, 128))
        pivots[first + j:first + j + 1, :] = column[j:j + 1]
        inverse = 1.0 / pivot
        at = local == j
        row = jnp.where(at, inverse, row * inverse)
        packed = jnp.where(sub == j, row, jnp.where(at, 0.0, packed) - column * row)
    return packed


def solve_kernel(hess_ref, grad_ref, side_ref, coef_ref, new_ref, objective_ref, a_ref, pivots):
    lane = iota((1, 256), 1)
    for m in range(4):
        one_sided = hess_ref[m]
        a_ref[m] = 0.5 * (one_sided + one_sided.T)
    for k in range(8):
        low = 32 * k
        blocks = [a_ref[m, low:low + 32, :] for m in range(4)]
        packed = jnp.concatenate([b[:, low:low + 32] for b in blocks], axis=1)
        inverse = invert_packed(packed, pivots, low)
        inside = (lane >= low) & (lane < low + 32)
        sign = jnp.where(lane < low, -1.0, 1.0)
        for m in range(4):
            own = inverse[:, 32 * m:32 * m + 32]
            wide = jnp.concatenate(
                ([jnp.zeros((32, low), F32)] if low else []) + [own]
                + ([jnp.zeros((32, 224 - low), F32)] if low < 224 else []),
                axis=1,
            )
            right = jnp.where(inside, wide, dot6(own, blocks[m], (((1,), (0,)), ((), ()))))
            change = dot6(blocks[m] * sign, right, TN)
            a_ref[m] = jnp.where(inside, 0.0, a_ref[m]) - change
            a_ref[m, low:low + 32, :] = right
    logs = jnp.sum(jnp.log(pivots[...]), axis=0, keepdims=True)
    side_lane = iota((1, 128), 1)
    for m in range(4):
        coef = coef_ref[m:m + 1, :]
        gradient = grad_ref[m] - LAMBDA * coef
        update = dot6(gradient, a_ref[m], (((1,), (0,)), ((), ())))
        new_ref[m:m + 1, :] = coef + update[0:1]
        half_logdet = 0.5 * jnp.sum(jnp.where(side_lane == 32 * m, logs, 0.0))
        mine = (side_lane >= 64 + 8 * m) & (side_lane < 72 + 8 * m)
        likelihood = jnp.sum(jnp.where(mine, side_ref[...], 0.0))
        objective_ref[m] = likelihood - 0.5 * LAMBDA * jnp.sum(coef * coef) - half_logdet


def solve(hess, grad, side_sum, coef):
    vmem = pl.BlockSpec(memory_space=pltpu.VMEM)
    return pl.pallas_call(
        solve_kernel,
        out_shape=(jax.ShapeDtypeStruct((4, 256), F32), jax.ShapeDtypeStruct((4,), F32)),
        in_specs=[vmem] * 4,
        out_specs=(vmem, pl.BlockSpec(memory_space=pltpu.SMEM)),
        scratch_shapes=[pltpu.VMEM((4, 256, 256), F32), pltpu.VMEM((256, 128), F32)],
        compiler_params=pltpu.CompilerParams(vmem_limit_bytes=32 * MIB),
        name="newton",
    )(hess, grad, side_sum, coef)


def margin_kernel(new_ref, z_ref, slot_ref, fixed_ref, out_ref, table, send_sem, recv_sem):
    me = position()
    barrier = pltpu.get_barrier_semaphore()
    peers = sum(ring_peers(me), [])
    for peer in peers:
        pl.semaphore_signal(barrier, inc=1, device_id=place(peer), device_id_type=MESH)
    table[pl.ds(pl.multiple_of(me * 8, 8), 8), :] = new_ref[...]
    pl.semaphore_wait(barrier, len(peers))
    for stage in range(3):
        gather_stage(table, me, stage, send_sem, recv_sem)()
    row_products(table, z_ref, slot_ref, out_ref)
    out_ref[...] += fixed_ref[...]


def margins(new8, z, slot, fixed):
    vmem = pl.BlockSpec(memory_space=pltpu.VMEM)
    return pl.pallas_call(
        margin_kernel,
        out_shape=jax.ShapeDtypeStruct((1, 2048), F32),
        in_specs=[vmem] * 4,
        out_specs=vmem,
        scratch_shapes=[
            pltpu.VMEM((1024, 128), F32),
            pltpu.SemaphoreType.DMA((3,)),
            pltpu.SemaphoreType.DMA((3,)),
        ],
        compiler_params=pltpu.CompilerParams(
            collective_id=1, has_side_effects=True, vmem_limit_bytes=32 * MIB
        ),
        name="margins",
    )(new8, z, slot, fixed)


def shards(feat_values, feat_blocks, fixed_coef, member_of, labels, re_features, member_slot, coef):
    hess, grad, side_sum, slot, fixed = dispatch(
        feat_values.reshape(16384, 128),
        feat_blocks.T,
        fixed_coef,
        member_of.reshape(1, 2048),
        labels.reshape(1, 2048),
        re_features,
        member_slot.reshape(1, 512),
        coef.reshape(8, 128),
    )
    new_coef, objective = solve(hess, grad, side_sum, coef)
    margin = margins(new_coef.reshape(8, 128), re_features, slot, fixed)
    return (new_coef, objective, margin.reshape(2048))


def solution(mesh):
    placed = (
        P("dp", "mp", None),
        P("dp", "mp"),
        P(),
        P(("dp", "mp"), None),
        P(("dp", "mp")),
        P(("dp", "mp"), None),
        P(),
        P(("dp", "mp"), None),
    )
    return jax.shard_map(
        shards,
        mesh=mesh,
        in_specs=placed,
        out_specs=(P(("dp", "mp"), None), P(("dp", "mp")), P(("dp", "mp"))),
        check_vma=False,
    )
```

```python
import functools

import jax
import jax.numpy as jnp
from jax import lax
from jax.experimental import pallas as pl
from jax.experimental.pallas import tpu as pltpu
from jax.sharding import PartitionSpec as P

R = 256
CAP = 8
LAMBDA = 1.0

MESH = pl.DeviceIdType.MESH
F32 = jnp.float32
BF16 = jnp.bfloat16
NT = (((1,), (1,)), ((), ()))
TN = (((0,), (0,)), ((), ()))
MIB = 1 << 20


def iota(shape, axis):
    return lax.broadcasted_iota(jnp.int32, shape, axis)


def halves(x):
    high = x.astype(BF16)
    return high, (x - high.astype(F32)).astype(BF16)


def thirds(x):
    high, rest = x.astype(BF16), None
    rest = x - high.astype(F32)
    middle = rest.astype(BF16)
    return high, middle, (rest - middle.astype(F32)).astype(BF16)


def place(device):
    return (device // 4, lax.rem(device, 4))


def position():
    return lax.axis_index("dp") * 4 + lax.axis_index("mp")


def one_hot(condition):
    return jnp.where(condition, 1.0, 0.0).astype(BF16)


def each_other(body):
    def some(i, carry):
        for j in range(8):
            body(1 + 8 * i + j)
        return carry

    lax.fori_loop(0, 15, some, 0)
    for k in range(121, 128):
        body(k)


def chip_and_core(me):
    return me // 8 * 4 + lax.rem(me, 4), lax.rem(me // 4, 2)


def table_place(me):
    chip, core = chip_and_core(me)
    return core * 64 + chip


def block_copy(table, blocks, peer, sem, number):
    return pltpu.make_async_remote_copy(
        src_ref=table.at[blocks],
        dst_ref=table.at[blocks],
        send_sem=sem.at[number],
        recv_sem=sem.at[2 + number],
        device_id=peer,
        device_id_type=MESH,
    )


def send_block(table, block, me, sem):
    chip, core = chip_and_core(me)
    at = table_place(me)
    table[pl.ds(at, 1)] = block.astype(BF16).reshape(1, 8, 128)

    def some(i, carry):
        for j in range(9):
            other = lax.rem(chip + (1 + 9 * i + j), 64)
            peer = (other // 4 * 2 + core, lax.rem(other, 4))
            block_copy(table, pl.ds(at, 1), peer, sem, 0).start()
        return carry

    lax.fori_loop(0, 7, some, 0)


def swap_blocks(table, me, sem):
    waiting = block_copy(table, pl.ds(0, 63), place(me), sem, 0)
    waiting.wait_send()
    waiting.wait_recv()
    _, core = chip_and_core(me)
    sibling = (me // 8 * 2 + 1 - core, lax.rem(me, 4))
    block_copy(table, pl.ds(core * 64, 64), sibling, sem, 1).start()


def finish_swap(table, wide, me, sem):
    waiting = block_copy(table, pl.ds(0, 64), place(me), sem, 1)
    waiting.wait_send()
    waiting.wait_recv()
    wide[...] = table[...].astype(F32).reshape(1024, 128)


def row_products(wide, z_ref, slot_ref, out_ref):
    half = [wide[pl.ds(h, 512, stride=2), :].astype(BF16) for h in range(2)]
    coefs = jnp.concatenate(half, axis=1)
    for c in range(8):
        lanes = pl.ds(256 * c, 256)
        product = lax.dot_general(coefs, z_ref[lanes, :], NT, preferred_element_type=F32)
        chosen = iota((512, 256), 0) == slot_ref[:, lanes]
        out_ref[:, lanes] = jnp.sum(jnp.where(chosen, product, 0.0), axis=0, keepdims=True)


def dispatch_kernel(
    v_hbm, ids_hbm, w_hbm, member_hbm, label_hbm, z_hbm, slots_hbm, coef_hbm,
    hess_ref, grad_ref, side_sum_ref, slot_ref, fixed_ref,
    v_ref, ids_ref, w_ref, member_ref, label_ref, z_ref, slots_ref, coef_ref,
    onehot, ids2, part, fixed_part, fixed_recv, table, wide, target_ref, score_ref,
    send, recv, side_send, side_recv,
    load_sem, table_sem, fixed_sem, side_sem, rows_send_sem, rows_recv_sem,
):
    me = position()
    mine = lax.axis_index("mp")
    group, inner = me // 8, lax.rem(me, 8)

    loads = [
        pltpu.make_async_copy(source, target, load_sem.at[n])
        for n, (source, target) in enumerate((
            (member_hbm, member_ref), (slots_hbm, slots_ref), (coef_hbm, coef_ref),
            (ids_hbm, ids_ref), (w_hbm, w_ref), (label_hbm, label_ref), (v_hbm, v_ref),
            (z_hbm, z_ref),
        ))
    ]
    for load in loads:
        load.start()

    barrier = pltpu.get_barrier_semaphore()

    def greet(k):
        peer = lax.rem(me + k, 128)
        pl.semaphore_signal(barrier, inc=1, device_id=place(peer), device_id_type=MESH)

    each_other(greet)

    loads[0].wait()
    loads[1].wait()
    for c in range(8):
        lanes = pl.ds(256 * c, 256)
        onehot[:, lanes] = one_hot(iota((512, 256), 0) == member_ref[:, lanes])
    slots = slots_ref[...]
    sub = iota((8, 512), 0)
    owner = slots // 4
    owner_row = jnp.where(sub == 1, lax.rem(slots, 4), jnp.where(sub == 2, table_place(owner), 0))
    owner_row = jnp.where(sub == 0, owner, owner_row).astype(F32).astype(BF16)
    before = one_hot(iota((256, 256), 0) < iota((256, 256), 1))
    tally = jnp.concatenate([before, jnp.ones((256, 256), BF16)], axis=1)
    base = jnp.zeros((512, 256), F32)
    for c in range(8):
        lanes = pl.ds(256 * c, 256)
        hot = onehot[:, lanes]
        found = jnp.dot(owner_row, hot, preferred_element_type=F32)
        counted = jnp.dot(hot, tally, preferred_element_type=F32)
        rank = jnp.sum(hot.astype(F32) * (base + counted[:, :256]), axis=0, keepdims=True)
        base = base + counted[:, 256:]
        slot_ref[:, lanes] = (found[2:3] * 4.0 + found[1:2]).astype(jnp.int32)
        target = found[0:1] * 32.0 + found[1:2] * 8.0 + rank
        target_ref[:, lanes] = target.astype(jnp.int32)

    for load in loads[2:]:
        load.wait()
    for r in range(64):
        for k in range(2):
            ids2[k, r:r + 1, :] = ids_ref[k:k + 1, 128 * r:128 * r + 128]
    spread = [one_hot(iota((128, 256), 1) == 2 * iota((128, 256), 0) + k) for k in range(2)]
    part[...] = sum(
        jnp.dot(ids2[k].astype(F32).astype(BF16), spread[k], preferred_element_type=F32)
        for k in range(2)
    )
    w2 = jnp.concatenate(halves(w_ref[...]), axis=1)

    def margin_rows(r, carry):
        rows = v_ref[pl.ds(pl.multiple_of(r * 256, 256), 256), :]
        product = lax.dot_general(
            w2, jnp.concatenate([rows, rows], axis=1), NT, preferred_element_type=F32
        )
        chosen = iota((128, 256), 0) == part[pl.ds(r, 1), :].astype(jnp.int32)
        part[pl.ds(r, 1), :] = jnp.sum(jnp.where(chosen, product, 0.0), axis=0, keepdims=True)
        return carry

    lax.fori_loop(0, 64, margin_rows, 0, unroll=4)
    pairs = one_hot(iota((256, 128), 0) // 2 == iota((256, 128), 1))
    fixed_part[...] = sum(
        jnp.dot(piece, pairs, preferred_element_type=F32) for piece in thirds(part[...])
    )

    pl.semaphore_wait(barrier, 127)
    for k in range(1, 4):
        other = lax.rem(mine + k, 4)
        pltpu.make_async_remote_copy(
            src_ref=fixed_part.at[pl.ds(pl.multiple_of(other * 16, 16), 16)],
            dst_ref=fixed_recv.at[pl.ds(k * 16, 16)],
            send_sem=fixed_sem.at[0],
            recv_sem=fixed_sem.at[1],
            device_id=(lax.axis_index("dp"), other),
            device_id_type=MESH,
        ).start()
    send_block(table, coef_ref[...], me, table_sem)

    def send_rows(phase, c):
        chunk = lax.rem(group + c, 16)
        target = target_ref[...] - chunk * 256
        picked = jnp.zeros((256, 256), F32)
        for piece in range(4):
            lanes = pl.ds(512 * piece, 512)
            hot = one_hot(iota((256, 512), 0) == target[:, 512 * piece:512 * piece + 512])
            picked = picked + jnp.dot(hot, z_ref[lanes, :], preferred_element_type=F32)
        send[pl.ds(chunk * 8, 8)] = picked.astype(BF16).reshape(8, 32, 256)

        def send_one(j):
            to = lax.rem(inner + j, 8)
            pltpu.make_async_remote_copy(
                src_ref=send.at[chunk * 8 + to],
                dst_ref=recv.at[me],
                send_sem=rows_send_sem,
                recv_sem=rows_recv_sem.at[phase],
                device_id=(chunk * 2 + to // 4, lax.rem(to, 4)),
                device_id_type=MESH,
            ).start()

        for j in range(1, 8):
            send_one(j)
        if isinstance(c, int) and c == 0:
            recv[pl.ds(me, 1)] = send[pl.ds(me, 1)]
        else:
            send_one(0)

    def send_phase(phase):
        def step(c, carry):
            send_rows(phase, c)
            return carry

        if phase == 0:
            send_rows(0, 0)
        lax.fori_loop(4 * phase + (phase == 0), 4 * phase + 4, step, 0)

    send_phase(0)
    send_phase(1)

    waiting = pltpu.make_async_remote_copy(
        src_ref=fixed_part.at[pl.ds(0, 48)],
        dst_ref=fixed_recv.at[pl.ds(16, 48)],
        send_sem=fixed_sem.at[0],
        recv_sem=fixed_sem.at[1],
        device_id=place(me),
        device_id_type=MESH,
    )
    waiting.wait_send()
    waiting.wait_recv()
    own = fixed_part[pl.ds(pl.multiple_of(mine * 16, 16), 16), :]
    total = own + fixed_recv[16:32] + fixed_recv[32:48] + fixed_recv[48:64]
    for r in range(16):
        fixed_ref[:, 128 * r:128 * r + 128] = total[r:r + 1, :]
    swap_blocks(table, me, table_sem)

    send_phase(2)

    finish_swap(table, wide, me, table_sem)
    row_products(wide, z_ref, slot_ref, score_ref)
    score = score_ref[...] + fixed_ref[...]
    label = label_ref[...].astype(F32)
    small = jnp.exp(-jnp.abs(score))
    probability = jnp.where(score >= 0.0, 1.0, small) / (1.0 + small)
    weight = small / ((1.0 + small) * (1.0 + small))
    residual = label - probability
    likelihood = label * score - (jnp.maximum(score, 0.0) + jnp.log1p(small))
    target = target_ref[...]
    total_side = jnp.zeros((128, 128), F32)
    for c in range(4):
        lanes = slice(512 * c, 512 * c + 512)
        owner_hot = one_hot(iota((128, 512), 0) == target[:, lanes] // 32)
        within = iota((32, 512), 0) == lax.rem(target[:, lanes], 32)
        sides = jnp.concatenate(
            [jnp.where(within, q[:, lanes], 0.0) for q in (weight, residual, likelihood)]
            + [jnp.zeros((32, 512), F32)],
            axis=0,
        )
        for piece in halves(sides):
            total_side = total_side + lax.dot_general(
                owner_hot, piece, NT, preferred_element_type=F32
            )
    for d in range(128):
        side_send[d] = total_side[d:d + 1, :]

    def side_copy(sources, targets, owner):
        return pltpu.make_async_remote_copy(
            src_ref=sources,
            dst_ref=targets,
            send_sem=side_sem.at[0],
            recv_sem=side_sem.at[1],
            device_id=place(owner),
            device_id_type=MESH,
        )

    def send_side(k):
        owner = lax.rem(me + k, 128)
        side_copy(side_send.at[owner], side_recv.at[me], owner).start()

    each_other(send_side)
    side_recv[pl.ds(me, 1)] = side_send[pl.ds(me, 1)]

    send_phase(3)

    waiting = side_copy(side_send.at[pl.ds(0, 127)], side_recv.at[pl.ds(0, 127)], me)
    waiting.wait_send()
    waiting.wait_recv()

    side_sum_ref[...] = jnp.sum(side_recv[...], axis=0)
    eye = jnp.where(iota((256, 256), 0) == iota((256, 256), 1), LAMBDA, 0.0)
    ones = jnp.ones((256, 128), BF16)
    lane = iota((32, 8, 128), 2) - iota((32, 8, 128), 1)
    for phase in range(4):
        count = 31 if phase == 0 else 32
        waiting = pltpu.make_async_remote_copy(
            src_ref=send.at[pl.ds(0, count)],
            dst_ref=recv.at[pl.ds(0, count)],
            send_sem=rows_send_sem,
            recv_sem=rows_recv_sem.at[phase],
            device_id=place(me),
            device_id_type=MESH,
        )
        waiting.wait_recv()
        starts = [lax.rem(group + 16 - (4 * phase + j), 16) * 8 for j in range(4)]
        sides = jnp.concatenate([side_recv[pl.ds(at, 8)] for at in starts], axis=0)
        sides = jnp.broadcast_to(sides, (32, 8, 128))
        for m in range(4):
            rows = jnp.concatenate(
                [recv[pl.ds(at, 8), 8 * m:8 * m + 8, :].astype(F32) for at in starts], axis=0
            ).reshape(256, 256)
            rows_b = rows.astype(BF16)
            column = []
            for quantity in range(2):
                chosen = lane == 32 * quantity + 8 * m
                picked = jnp.where(chosen, sides, 0.0).reshape(256, 128)
                picked = jnp.concatenate(halves(picked), axis=1)
                column.append(jnp.dot(picked, ones, preferred_element_type=F32))
            weights = jnp.concatenate([column[0], column[0]], axis=1)
            weighted = (weights * rows).astype(BF16)
            update = lax.dot_general(weighted, rows_b, TN, preferred_element_type=F32)
            pull = lax.dot_general(
                column[1].astype(BF16), rows_b, TN, preferred_element_type=F32
            )[0:8]
            if phase == 0:
                hess_ref[m] = eye + update
                grad_ref[m] = pull
            else:
                hess_ref[m] += update
                grad_ref[m] += pull
    waiting = pltpu.make_async_remote_copy(
        src_ref=send.at[pl.ds(0, 127)],
        dst_ref=recv.at[pl.ds(0, 127)],
        send_sem=rows_send_sem,
        recv_sem=rows_recv_sem.at[0],
        device_id=place(me),
        device_id_type=MESH,
    )
    waiting.wait_send()


def dispatch(v, ids, fixed_coef, member, labels, z, slots, coef8):
    vmem = pl.BlockSpec(memory_space=pltpu.VMEM)
    operands = (v, ids, fixed_coef, member, labels, z, slots, coef8)
    return pl.pallas_call(
        dispatch_kernel,
        out_shape=(
            jax.ShapeDtypeStruct((4, 256, 256), F32),
            jax.ShapeDtypeStruct((4, 8, 256), F32),
            jax.ShapeDtypeStruct((1, 128), F32),
            jax.ShapeDtypeStruct((1, 2048), jnp.int32),
            jax.ShapeDtypeStruct((1, 2048), F32),
        ),
        in_specs=[pl.BlockSpec(memory_space=pl.ANY)] * 8,
        out_specs=(vmem,) * 5,
        scratch_shapes=[pltpu.VMEM(x.shape, x.dtype) for x in operands] + [
            pltpu.VMEM((512, 2048), BF16),
            pltpu.VMEM((2, 64, 128), jnp.int32),
            pltpu.VMEM((64, 256), F32),
            pltpu.VMEM((64, 128), F32),
            pltpu.VMEM((64, 128), F32),
            pltpu.VMEM((128, 8, 128), BF16),
            pltpu.VMEM((1024, 128), F32),
            pltpu.VMEM((1, 2048), jnp.int32),
            pltpu.VMEM((1, 2048), F32),
            pltpu.VMEM((128, 32, 256), BF16),
            pltpu.VMEM((128, 32, 256), BF16),
            pltpu.VMEM((128, 1, 128), F32),
            pltpu.VMEM((128, 1, 128), F32),
            pltpu.SemaphoreType.DMA((8,)),
            pltpu.SemaphoreType.DMA((4,)),
            pltpu.SemaphoreType.DMA((2,)),
            pltpu.SemaphoreType.DMA((2,)),
            pltpu.SemaphoreType.DMA,
            pltpu.SemaphoreType.DMA((4,)),
        ],
        compiler_params=pltpu.CompilerParams(
            collective_id=0, has_side_effects=True, vmem_limit_bytes=56 * MIB
        ),
        name="dispatch",
    )(*operands)


def six_left(x, axis=0):
    high, middle, low = thirds(x)
    return jnp.concatenate([high, high, middle, middle, high, low], axis=axis)


def six_right(x, axis=0):
    high, middle, low = thirds(x)
    return jnp.concatenate([high, middle, high, middle, low, high], axis=axis)


def dot6(left, right, dims):
    ((la,), (ra,)), _ = dims
    return lax.dot_general(
        six_left(left, la), six_right(right, ra), dims, preferred_element_type=F32
    )


def factor_packed(packed, pivots, first, between):
    lane = iota((32, 128), 1)
    group = lane // 32 * 32
    local = lane - group
    sub = iota((32, 128), 0)
    local1 = local[0:1]
    roots = jnp.zeros((32, 128), F32)
    for j in range(0, 32, 4):
        below = sub >= j + 4
        columns = [
            jnp.take_along_axis(packed, group + (j + a), axis=1, mode="promise_in_bounds")
            for a in range(4)
        ]
        p = {(a, b): columns[b][j + a:j + a + 1] for a in range(4) for b in range(a, 4)}
        inside = (local1 >= j) & (local1 < j + 4)
        rows = [
            jnp.where(inside, jnp.where(local1 == j + a, 1.0, 0.0), packed[j + a:j + a + 1])
            for a in range(4)
        ]
        change = jnp.zeros((32, 128), F32)
        for a in range(4):
            scale = 1.0 / p[a, a]
            for b in range(a + 1, 4):
                ratio = p[a, b] * scale
                for c in range(b, 4):
                    p[b, c] = p[b, c] - ratio * p[a, c]
                rows[b] = rows[b] - ratio * rows[a]
                columns[b] = columns[b] - columns[a] * ratio
            change = change + columns[a] * (rows[a] * scale)
            pivots[first + j + a:first + j + a + 1, :] = p[a, a]
        kept = jnp.where((local >= j) & (local < j + 4), 0.0, packed) - change
        packed = jnp.where(below, kept, packed)
        for a in range(4):
            packed = jnp.where(sub == j + a, rows[a], packed)
            roots = jnp.where(sub == j + a, lax.rsqrt(p[a, a]), roots)
        between()
    return jnp.where(local <= sub, packed, 0.0) * roots


def solve_kernel(hess_ref, grad_ref, side_ref, coef_ref, new_ref, objective_ref, a_ref, pivots):
    lane = iota((1, 256), 1)
    for m in range(4):
        one_sided = hess_ref[m]
        a_ref[m] = 0.5 * (one_sided + one_sided.T)
    blocks = [a_ref[m, 0:32, :] for m in range(4)]
    pending = []

    def between():
        if pending:
            pending.pop(0)()

    for k in range(8):
        low = 32 * k
        packed = jnp.concatenate([b[:, low:low + 32] for b in blocks], axis=1)
        inverse = factor_packed(packed, pivots, low, between)
        while pending:
            between()
        inside = (lane >= low) & (lane < low + 32)
        sign = jnp.where(lane < low, -1.0, 1.0)
        following = []
        for m in range(4):
            own = inverse[:, 32 * m:32 * m + 32]
            wide = jnp.concatenate(
                ([jnp.zeros((32, low), F32)] if low else []) + [own]
                + ([jnp.zeros((32, 224 - low), F32)] if low < 224 else []),
                axis=1,
            )
            half = jnp.where(inside, wide, dot6(own, blocks[m], (((1,), (0,)), ((), ()))))
            left = six_left(half * sign)
            right = six_right(half)
            skipped = [k]
            if k < 7:
                change = lax.dot_general(
                    left[:, low + 32:low + 64], right, TN, preferred_element_type=F32
                )
                ahead = jnp.where(inside, 0.0, a_ref[m, low + 32:low + 64, :]) - change
                following.append(ahead)
                a_ref[m, low + 32:low + 64, :] = ahead
                skipped.append(k + 1)

            def bulk(part, m=m, low=low, own=own, left=left, right=right, inside=inside,
                     skipped=skipped):
                change = lax.dot_general(
                    left[:, 128 * part:128 * part + 128], right, TN, preferred_element_type=F32
                )
                for n in range(4):
                    if 4 * part + n not in skipped:
                        rows = slice(128 * part + 32 * n, 128 * part + 32 * n + 32)
                        a_ref[m, rows, :] = (
                            jnp.where(inside, 0.0, a_ref[m, rows, :]) - change[32 * n:32 * n + 32]
                        )
                if part == 1:
                    a_ref[m, low:low + 32, :] = lax.dot_general(
                        six_left(own), right, TN, preferred_element_type=F32
                    )

            pending += [functools.partial(bulk, part) for part in range(2)]
        blocks = following
    while pending:
        between()
    logs = jnp.sum(jnp.log(pivots[...]), axis=0, keepdims=True)
    side_lane = iota((1, 128), 1)
    for m in range(4):
        coef = coef_ref[m:m + 1, :]
        gradient = grad_ref[m] - LAMBDA * coef
        update = dot6(gradient, a_ref[m], (((1,), (0,)), ((), ())))
        new_ref[m:m + 1, :] = coef + update[0:1]
        half_logdet = 0.5 * jnp.sum(jnp.where(side_lane == 32 * m, logs, 0.0))
        mine = (side_lane >= 64 + 8 * m) & (side_lane < 72 + 8 * m)
        likelihood = jnp.sum(jnp.where(mine, side_ref[...], 0.0))
        objective_ref[m] = likelihood - 0.5 * LAMBDA * jnp.sum(coef * coef) - half_logdet


def solve(hess, grad, side_sum, coef):
    vmem = pl.BlockSpec(memory_space=pltpu.VMEM)
    return pl.pallas_call(
        solve_kernel,
        out_shape=(jax.ShapeDtypeStruct((4, 256), F32), jax.ShapeDtypeStruct((4,), F32)),
        in_specs=[vmem] * 4,
        out_specs=(vmem, pl.BlockSpec(memory_space=pltpu.SMEM)),
        scratch_shapes=[pltpu.VMEM((4, 256, 256), F32), pltpu.VMEM((256, 128), F32)],
        compiler_params=pltpu.CompilerParams(vmem_limit_bytes=32 * MIB),
        name="newton",
    )(hess, grad, side_sum, coef)


def margin_kernel(new_ref, z_ref, slot_ref, fixed_ref, out_ref, table, wide, sem):
    me = position()
    chip, core = chip_and_core(me)
    barrier = pltpu.get_barrier_semaphore()

    def greet(i, carry):
        for j in range(9):
            other = lax.rem(chip + (1 + 9 * i + j), 64)
            peer = (other // 4 * 2 + core, lax.rem(other, 4))
            pl.semaphore_signal(barrier, inc=1, device_id=peer, device_id_type=MESH)
        return carry

    lax.fori_loop(0, 7, greet, 0)
    sibling = (me // 8 * 2 + 1 - core, lax.rem(me, 4))
    pl.semaphore_signal(barrier, inc=1, device_id=sibling, device_id_type=MESH)
    pl.semaphore_wait(barrier, 64)
    send_block(table, new_ref[...], me, sem)
    swap_blocks(table, me, sem)
    finish_swap(table, wide, me, sem)
    row_products(wide, z_ref, slot_ref, out_ref)
    out_ref[...] += fixed_ref[...]


def margins(new8, z, slot, fixed):
    vmem = pl.BlockSpec(memory_space=pltpu.VMEM)
    return pl.pallas_call(
        margin_kernel,
        out_shape=jax.ShapeDtypeStruct((1, 2048), F32),
        in_specs=[vmem] * 4,
        out_specs=vmem,
        scratch_shapes=[
            pltpu.VMEM((128, 8, 128), BF16),
            pltpu.VMEM((1024, 128), F32),
            pltpu.SemaphoreType.DMA((4,)),
        ],
        compiler_params=pltpu.CompilerParams(
            collective_id=1, has_side_effects=True, vmem_limit_bytes=32 * MIB
        ),
        name="margins",
    )(new8, z, slot, fixed)


def shards(feat_values, feat_blocks, fixed_coef, member_of, labels, re_features, member_slot, coef):
    hess, grad, side_sum, slot, fixed = dispatch(
        feat_values.reshape(16384, 128),
        feat_blocks.T,
        fixed_coef,
        member_of.reshape(1, 2048),
        labels.reshape(1, 2048),
        re_features,
        member_slot.reshape(1, 512),
        coef.reshape(8, 128),
    )
    new_coef, objective = solve(hess, grad, side_sum, coef)
    margin = margins(new_coef.reshape(8, 128), re_features, slot, fixed)
    return (new_coef, objective, margin.reshape(2048))


def solution(mesh):
    placed = (
        P("dp", "mp", None),
        P("dp", "mp"),
        P(),
        P(("dp", "mp"), None),
        P(("dp", "mp")),
        P(("dp", "mp"), None),
        P(),
        P(("dp", "mp"), None),
    )
    return jax.shard_map(
        shards,
        mesh=mesh,
        in_specs=placed,
        out_specs=(P(("dp", "mp"), None), P(("dp", "mp")), P(("dp", "mp"))),
        check_vma=False,
    )
```

```python
import functools

import jax
import jax.numpy as jnp
from jax import lax
from jax.experimental import pallas as pl
from jax.experimental.pallas import tpu as pltpu
from jax.sharding import PartitionSpec as P

R = 256
CAP = 8
LAMBDA = 1.0

MESH = pl.DeviceIdType.MESH
F32 = jnp.float32
BF16 = jnp.bfloat16
NT = (((1,), (1,)), ((), ()))
TN = (((0,), (0,)), ((), ()))
MIB = 1 << 20


def iota(shape, axis):
    return lax.broadcasted_iota(jnp.int32, shape, axis)


def halves(x):
    high = x.astype(BF16)
    return high, (x - high.astype(F32)).astype(BF16)


def thirds(x):
    high, rest = x.astype(BF16), None
    rest = x - high.astype(F32)
    middle = rest.astype(BF16)
    return high, middle, (rest - middle.astype(F32)).astype(BF16)


def one_hot(condition):
    return jnp.where(condition, 1.0, 0.0).astype(BF16)


class Torus:
    def __init__(self):
        dp, self.y = lax.axis_index("dp"), lax.axis_index("mp")
        self.z, self.x, self.core = dp // 8, lax.rem(dp // 2, 4), lax.rem(dp, 2)
        self.zs = [lax.rem(self.z + d, 4) * 8 for d in range(4)]
        self.xs = [lax.rem(self.x + d, 4) * 2 for d in range(4)]
        self.cores = [self.core, 1 - self.core]
        self.ys = [lax.rem(self.y + d, 4) for d in range(4)]

    def peer(self, k):
        digits = 77 * k % 128
        dp = self.zs[digits // 32] + self.xs[digits // 8 % 4] + self.cores[digits // 4 % 2]
        return dp, self.ys[digits % 4]

    def step_of(self, owner):
        dz = lax.rem(owner // 32 + (4 - self.z), 4)
        dx = lax.rem(lax.rem(owner // 8, 4) + (4 - self.x), 4)
        core = lax.rem(lax.rem(owner // 4, 2) + (2 - self.core), 2)
        dy = lax.rem(lax.rem(owner, 4) + (4 - self.y), 4)
        return lax.rem(5 * (dz * 32 + dx * 8 + core * 4 + dy), 128)

    def chip_peer(self, k):
        digits = 29 * k % 64
        dp = self.zs[digits // 16] + self.xs[digits // 4 % 4] + self.core
        return dp, self.ys[digits % 4]

    def sibling(self):
        return self.zs[0] + self.xs[0] + self.cores[1], self.y

    def table_place(self):
        return self.core * 64 + self.z * 16 + self.x * 4 + self.y


def table_place(device):
    return lax.rem(device // 4, 2) * 64 + device // 8 * 4 + lax.rem(device, 4)


def remote(source, target, send_sem, recv_sem, peer):
    return pltpu.make_async_remote_copy(
        src_ref=source,
        dst_ref=target,
        send_sem=send_sem,
        recv_sem=recv_sem,
        device_id=peer,
        device_id_type=MESH,
    )


def row_products(wide, z_ref, slot_ref, out_ref):
    half = [wide[pl.ds(h, 512, stride=2), :].astype(BF16) for h in range(2)]
    coefs = jnp.concatenate(half, axis=1)
    for c in range(8):
        lanes = pl.ds(256 * c, 256)
        product = lax.dot_general(coefs, z_ref[lanes, :], NT, preferred_element_type=F32)
        chosen = iota((512, 256), 0) == slot_ref[:, lanes]
        out_ref[:, lanes] = jnp.sum(jnp.where(chosen, product, 0.0), axis=0, keepdims=True)


def six_left(x, axis=0):
    high, middle, low = thirds(x)
    return jnp.concatenate([high, high, middle, middle, high, low], axis=axis)


def six_right(x, axis=0):
    high, middle, low = thirds(x)
    return jnp.concatenate([high, middle, high, middle, low, high], axis=axis)


def dot6(left, right, dims):
    ((la,), (ra,)), _ = dims
    return lax.dot_general(
        six_left(left, la), six_right(right, ra), dims, preferred_element_type=F32
    )


def factor_packed(packed, pivots, first, between):
    lane = iota((32, 128), 1)
    group = lane // 32 * 32
    local = lane - group
    sub = iota((32, 128), 0)
    local1 = local[0:1]
    roots = jnp.zeros((32, 128), F32)
    for j in range(0, 32, 4):
        below = sub >= j + 4
        columns = [
            jnp.take_along_axis(packed, group + (j + a), axis=1, mode="promise_in_bounds")
            for a in range(4)
        ]
        p = {(a, b): columns[b][j + a:j + a + 1] for a in range(4) for b in range(a, 4)}
        inside = (local1 >= j) & (local1 < j + 4)
        rows = [
            jnp.where(inside, jnp.where(local1 == j + a, 1.0, 0.0), packed[j + a:j + a + 1])
            for a in range(4)
        ]
        change = jnp.zeros((32, 128), F32)
        for a in range(4):
            scale = 1.0 / p[a, a]
            for b in range(a + 1, 4):
                ratio = p[a, b] * scale
                for c in range(b, 4):
                    p[b, c] = p[b, c] - ratio * p[a, c]
                rows[b] = rows[b] - ratio * rows[a]
                columns[b] = columns[b] - columns[a] * ratio
            change = change + columns[a] * (rows[a] * scale)
            pivots[first + j + a:first + j + a + 1, :] = p[a, a]
        kept = jnp.where((local >= j) & (local < j + 4), 0.0, packed) - change
        packed = jnp.where(below, kept, packed)
        for a in range(4):
            packed = jnp.where(sub == j + a, rows[a], packed)
            roots = jnp.where(sub == j + a, lax.rsqrt(p[a, a]), roots)
        between()
    return jnp.where(local <= sub, packed, 0.0) * roots


def newton(a_ref, grad_ref, likelihood_ref, coef_ref, new_ref, objective_ref, pivots):
    lane = iota((1, 256), 1)
    for m in range(4):
        one_sided = a_ref[m]
        a_ref[m] = 0.5 * (one_sided + one_sided.T)
    blocks = [a_ref[m, 0:32, :] for m in range(4)]
    pending = []

    def between():
        if pending:
            pending.pop(0)()

    for k in range(8):
        low = 32 * k
        packed = jnp.concatenate([b[:, low:low + 32] for b in blocks], axis=1)
        inverse = factor_packed(packed, pivots, low, between)
        while pending:
            between()
        inside = (lane >= low) & (lane < low + 32)
        sign = jnp.where(lane < low, -1.0, 1.0)
        following = []
        for m in range(4):
            own = inverse[:, 32 * m:32 * m + 32]
            wide = jnp.concatenate(
                ([jnp.zeros((32, low), F32)] if low else []) + [own]
                + ([jnp.zeros((32, 224 - low), F32)] if low < 224 else []),
                axis=1,
            )
            half = jnp.where(inside, wide, dot6(own, blocks[m], (((1,), (0,)), ((), ()))))
            left = six_left(half * sign)
            right = six_right(half)
            skipped = [k]
            if k < 7:
                change = lax.dot_general(
                    left[:, low + 32:low + 64], right, TN, preferred_element_type=F32
                )
                ahead = jnp.where(inside, 0.0, a_ref[m, low + 32:low + 64, :]) - change
                following.append(ahead)
                a_ref[m, low + 32:low + 64, :] = ahead
                skipped.append(k + 1)

            def bulk(part, m=m, low=low, own=own, left=left, right=right, inside=inside,
                     skipped=skipped):
                change = lax.dot_general(
                    left[:, 128 * part:128 * part + 128], right, TN, preferred_element_type=F32
                )
                for n in range(4):
                    if 4 * part + n not in skipped:
                        rows = slice(128 * part + 32 * n, 128 * part + 32 * n + 32)
                        a_ref[m, rows, :] = (
                            jnp.where(inside, 0.0, a_ref[m, rows, :]) - change[32 * n:32 * n + 32]
                        )
                if part == 1:
                    a_ref[m, low:low + 32, :] = lax.dot_general(
                        six_left(own), right, TN, preferred_element_type=F32
                    )

            pending += [functools.partial(bulk, part) for part in range(2)]
        blocks = following
    while pending:
        between()
    logs = jnp.sum(jnp.log(pivots[...]), axis=0, keepdims=True)
    side_lane = iota((1, 128), 1)
    news = []
    for m in range(4):
        coef = coef_ref[m:m + 1, :]
        gradient = grad_ref[m] - LAMBDA * coef
        update = dot6(gradient, a_ref[m], (((1,), (0,)), ((), ())))
        new = coef + update[0:1]
        new_ref[m:m + 1, :] = new
        news += [new[:, :128], new[:, 128:]]
        logs_here = jnp.where(side_lane == 32 * m, logs, 0.0)
        half_logdet = 0.5 * jnp.sum(logs_here, axis=1, keepdims=True)
        square = jnp.sum(coef * coef, axis=1, keepdims=True)
        objective_ref[m:m + 1, :] = (
            likelihood_ref[m:m + 1, :] - 0.5 * LAMBDA * square - half_logdet
        )
    return jnp.concatenate(news, axis=0)


def step_kernel(
    v_hbm, ids_hbm, w_hbm, member_hbm, label_hbm, z_hbm, slots_hbm, coef_hbm,
    new_ref, objective_ref, margin_ref,
    v_ref, ids_ref, w_ref, member_ref, label_ref, z_ref, slots_ref, coef_ref,
    onehot, ids2, part, fixed_part, fixed_recv, fixed_ref, table, wide, target_ref, slot_ref,
    send, recv, side_send, side_recv, a_ref, grad_ref, likelihood_ref, pivots,
    load_sem, table_sem, fixed_sem, side_sem, rows_send_sem, rows_recv_sem,
):
    torus = Torus()

    loads = [
        pltpu.make_async_copy(source, target, load_sem.at[n])
        for n, (source, target) in enumerate((
            (member_hbm, member_ref), (slots_hbm, slots_ref), (coef_hbm, coef_ref),
            (ids_hbm, ids_ref), (w_hbm, w_ref), (label_hbm, label_ref), (v_hbm, v_ref),
            (z_hbm, z_ref),
        ))
    ]
    for load in loads:
        load.start()

    barrier = pltpu.get_barrier_semaphore()
    greeted = iter(range(1, 128))

    def greet(count):
        for _ in range(count):
            k = next(greeted, None)
            if k is not None:
                pl.semaphore_signal(
                    barrier, inc=1, device_id=torus.peer(k), device_id_type=MESH
                )

    loads[0].wait()
    loads[1].wait()
    for c in range(8):
        lanes = pl.ds(256 * c, 256)
        onehot[:, lanes] = one_hot(iota((512, 256), 0) == member_ref[:, lanes])
        greet(8)
    slots = slots_ref[...]
    sub = iota((8, 512), 0)
    owner = slots // 4
    owner_row = jnp.where(sub == 1, lax.rem(slots, 4), jnp.where(sub == 2, table_place(owner), 0))
    owner_row = jnp.where(sub == 0, torus.step_of(owner), owner_row).astype(F32).astype(BF16)
    before = one_hot(iota((256, 256), 0) < iota((256, 256), 1))
    tally = jnp.concatenate([before, jnp.ones((256, 256), BF16)], axis=1)
    base = jnp.zeros((512, 256), F32)
    for c in range(8):
        lanes = pl.ds(256 * c, 256)
        hot = onehot[:, lanes]
        found = jnp.dot(owner_row, hot, preferred_element_type=F32)
        counted = jnp.dot(hot, tally, preferred_element_type=F32)
        rank = jnp.sum(hot.astype(F32) * (base + counted[:, :256]), axis=0, keepdims=True)
        base = base + counted[:, 256:]
        slot_ref[:, lanes] = (found[2:3] * 4.0 + found[1:2]).astype(jnp.int32)
        target = found[0:1] * 32.0 + found[1:2] * 8.0 + rank
        target_ref[:, lanes] = target.astype(jnp.int32)
        greet(8)

    for load in loads[2:]:
        load.wait()
    for r in range(64):
        for k in range(2):
            ids2[k, r:r + 1, :] = ids_ref[k:k + 1, 128 * r:128 * r + 128]
    spread = [one_hot(iota((128, 256), 1) == 2 * iota((128, 256), 0) + k) for k in range(2)]
    part[...] = sum(
        jnp.dot(ids2[k].astype(F32).astype(BF16), spread[k], preferred_element_type=F32)
        for k in range(2)
    )
    w2 = jnp.concatenate(halves(w_ref[...]), axis=1)

    def margin_rows(r, carry):
        rows = v_ref[pl.ds(pl.multiple_of(r * 256, 256), 256), :]
        product = lax.dot_general(
            w2, jnp.concatenate([rows, rows], axis=1), NT, preferred_element_type=F32
        )
        chosen = iota((128, 256), 0) == part[pl.ds(r, 1), :].astype(jnp.int32)
        part[pl.ds(r, 1), :] = jnp.sum(jnp.where(chosen, product, 0.0), axis=0, keepdims=True)
        return carry

    lax.fori_loop(0, 64, margin_rows, 0, unroll=4)
    pairs = one_hot(iota((256, 128), 0) // 2 == iota((256, 128), 1))
    fixed_part[...] = sum(
        jnp.dot(piece, pairs, preferred_element_type=F32) for piece in thirds(part[...])
    )

    def pick_rows(c, carry):
        target = target_ref[...] - c * 256
        picked = jnp.zeros((256, 256), F32)
        for piece in range(4):
            lanes = pl.ds(512 * piece, 512)
            hot = one_hot(iota((256, 512), 0) == target[:, 512 * piece:512 * piece + 512])
            picked = picked + jnp.dot(hot, z_ref[lanes, :], preferred_element_type=F32)
        send[pl.ds(c * 8, 8)] = picked.astype(BF16).reshape(8, 32, 256)
        return carry

    def row_copy(places, k, phase):
        return remote(
            send.at[places], recv.at[places], rows_send_sem, rows_recv_sem.at[phase],
            torus.peer(k),
        )

    def send_rows(phase):
        for k in range(max(32 * phase, 1), 32 * phase + 32):
            row_copy(k, k, phase).start()

    lax.fori_loop(0, 4, pick_rows, 0)
    pl.semaphore_wait(barrier, 127)
    for k in range(1, 4):
        remote(
            fixed_part.at[pl.ds(pl.multiple_of(torus.ys[k] * 16, 16), 16)],
            fixed_recv.at[pl.ds(k * 16, 16)],
            fixed_sem.at[0], fixed_sem.at[1],
            (lax.axis_index("dp"), torus.ys[k]),
        ).start()
    send_rows(0)
    lax.fori_loop(4, 8, pick_rows, 0)
    send_rows(1)
    recv[0] = send[0]

    waiting = remote(
        fixed_part.at[pl.ds(0, 48)], fixed_recv.at[pl.ds(16, 48)],
        fixed_sem.at[0], fixed_sem.at[1], torus.peer(0),
    )
    waiting.wait_send()
    waiting.wait_recv()
    own = fixed_part[pl.ds(pl.multiple_of(torus.y * 16, 16), 16), :]
    total = own + fixed_recv[16:32] + fixed_recv[32:48] + fixed_recv[48:64]
    for r in range(16):
        fixed_ref[:, 128 * r:128 * r + 128] = total[r:r + 1, :]
    fixed = fixed_ref[...]
    code = label_ref[...].astype(F32) + 1.0
    target = target_ref[...]
    sides = jnp.zeros((128, 128), F32)
    for c in range(4):
        lanes = slice(512 * c, 512 * c + 512)
        step_hot = one_hot(iota((128, 512), 0) == target[:, lanes] // 32)
        within = iota((32, 512), 0) == lax.rem(target[:, lanes], 32)
        values = jnp.concatenate(
            [jnp.where(within, q[:, lanes], 0.0) for q in (fixed, code)]
            + [jnp.zeros((64, 512), F32)],
            axis=0,
        )
        for piece in thirds(values):
            sides = sides + lax.dot_general(step_hot, piece, NT, preferred_element_type=F32)
    for k in range(128):
        side_send[k] = sides[k:k + 1, :]

    def side_copy(places, k):
        return remote(
            side_send.at[places], side_recv.at[places], side_sem.at[0], side_sem.at[1],
            torus.peer(k),
        )

    for k in range(1, 128):
        side_copy(k, k).start()
    side_recv[0] = side_send[0]

    for phase in (2, 3):
        lax.fori_loop(4 * phase, 4 * phase + 4, pick_rows, 0)
        send_rows(phase)

    waiting = side_copy(pl.ds(0, 127), 0)
    waiting.wait_send()
    waiting.wait_recv()
    eye = jnp.where(iota((256, 256), 0) == iota((256, 256), 1), LAMBDA, 0.0)
    ones = jnp.ones((256, 128), BF16)
    lane = iota((32, 8, 128), 2) - iota((32, 8, 128), 1)
    for phase in range(4):
        row_copy(pl.ds(0, 31 if phase == 0 else 32), 0, phase).wait_recv()
        here = slice(32 * phase, 32 * phase + 32)
        sides = jnp.broadcast_to(side_recv[here], (32, 8, 128))
        for m in range(4):
            rows = recv[here, 8 * m:8 * m + 8, :].astype(F32).reshape(256, 256)
            rows_b = rows.astype(BF16)
            coef_b = jnp.broadcast_to(coef_ref[m:m + 1, :], (128, 256)).astype(BF16)
            known = jnp.where(lane == 8 * m, sides, 0.0).reshape(256, 128)
            known = jnp.concatenate(halves(known), axis=1)
            score = lax.dot_general(rows_b, coef_b, NT, preferred_element_type=F32)
            score = score + jnp.dot(known, ones, preferred_element_type=F32)
            code = jnp.where(lane == 32 + 8 * m, sides, 0.0).reshape(256, 128)
            code = jnp.dot(code.astype(BF16), ones[:128], preferred_element_type=F32)
            live = code > 0.5
            label = code - 1.0
            small = jnp.exp(-jnp.abs(score))
            inverse = 1.0 / (1.0 + small)
            probability = jnp.where(score >= 0.0, 1.0, small) * inverse
            weight = jnp.where(live, small * inverse * inverse, 0.0)
            residual = jnp.where(live, label - probability, 0.0).astype(BF16)
            gain = label * score - (jnp.maximum(score, 0.0) + jnp.log1p(small))
            gain = jnp.sum(jnp.where(live, gain, 0.0), axis=0, keepdims=True)
            weighted = (jnp.concatenate([weight, weight], axis=1) * rows).astype(BF16)
            update = lax.dot_general(weighted, rows_b, TN, preferred_element_type=F32)
            pull = lax.dot_general(residual, rows_b, TN, preferred_element_type=F32)[0:8]
            if phase == 0:
                a_ref[m] = eye + update
                grad_ref[m] = pull
                likelihood_ref[m:m + 1, :] = gain
            else:
                a_ref[m] += update
                grad_ref[m] += pull
                likelihood_ref[m:m + 1, :] += gain

    block = newton(a_ref, grad_ref, likelihood_ref, coef_ref, new_ref, objective_ref, pivots)
    row_copy(pl.ds(0, 127), 0, 0).wait_send()

    at = torus.table_place()
    table[pl.ds(at, 1)] = block.astype(BF16).reshape(1, 8, 128)

    def table_copy(blocks, number, peer):
        return remote(
            table.at[blocks], table.at[blocks], table_sem.at[number], table_sem.at[2 + number],
            peer,
        )

    for k in range(1, 64):
        table_copy(pl.ds(at, 1), 0, torus.chip_peer(k)).start()
    waiting = table_copy(pl.ds(0, 63), 0, torus.sibling())
    waiting.wait_send()
    waiting.wait_recv()
    swap = table_copy(pl.ds(torus.core * 64, 64), 1, torus.sibling())
    swap.start()
    swap.wait_send()
    swap.wait_recv()
    wide[...] = table[...].astype(F32).reshape(1024, 128)
    row_products(wide, z_ref, slot_ref, margin_ref)
    margin_ref[...] += fixed_ref[...]


def step(v, ids, fixed_coef, member, labels, z, slots, coef):
    vmem = pl.BlockSpec(memory_space=pltpu.VMEM)
    operands = (v, ids, fixed_coef, member, labels, z, slots, coef)
    return pl.pallas_call(
        step_kernel,
        out_shape=(
            jax.ShapeDtypeStruct((4, 256), F32),
            jax.ShapeDtypeStruct((4, 128), F32),
            jax.ShapeDtypeStruct((1, 2048), F32),
        ),
        in_specs=[pl.BlockSpec(memory_space=pl.ANY)] * 8,
        out_specs=(vmem,) * 3,
        scratch_shapes=[pltpu.VMEM(x.shape, x.dtype) for x in operands] + [
            pltpu.VMEM((512, 2048), BF16),
            pltpu.VMEM((2, 64, 128), jnp.int32),
            pltpu.VMEM((64, 256), F32),
            pltpu.VMEM((64, 128), F32),
            pltpu.VMEM((64, 128), F32),
            pltpu.VMEM((1, 2048), F32),
            pltpu.VMEM((128, 8, 128), BF16),
            pltpu.VMEM((1024, 128), F32),
            pltpu.VMEM((1, 2048), jnp.int32),
            pltpu.VMEM((1, 2048), jnp.int32),
            pltpu.VMEM((128, 32, 256), BF16),
            pltpu.VMEM((128, 32, 256), BF16),
            pltpu.VMEM((128, 1, 128), F32),
            pltpu.VMEM((128, 1, 128), F32),
            pltpu.VMEM((4, 256, 256), F32),
            pltpu.VMEM((4, 8, 256), F32),
            pltpu.VMEM((4, 128), F32),
            pltpu.VMEM((256, 128), F32),
            pltpu.SemaphoreType.DMA((8,)),
            pltpu.SemaphoreType.DMA((4,)),
            pltpu.SemaphoreType.DMA((2,)),
            pltpu.SemaphoreType.DMA((2,)),
            pltpu.SemaphoreType.DMA,
            pltpu.SemaphoreType.DMA((4,)),
        ],
        compiler_params=pltpu.CompilerParams(
            collective_id=0, has_side_effects=True, vmem_limit_bytes=56 * MIB
        ),
        name="step",
    )(*operands)


def shards(feat_values, feat_blocks, fixed_coef, member_of, labels, re_features, member_slot, coef):
    new_coef, objective, margin = step(
        feat_values.reshape(16384, 128),
        feat_blocks.T,
        fixed_coef,
        member_of.reshape(1, 2048),
        labels.reshape(1, 2048),
        re_features,
        member_slot.reshape(1, 512),
        coef,
    )
    return (new_coef, objective[:, 0], margin.reshape(2048))


def solution(mesh):
    placed = (
        P("dp", "mp", None),
        P("dp", "mp"),
        P(),
        P(("dp", "mp"), None),
        P(("dp", "mp")),
        P(("dp", "mp"), None),
        P(),
        P(("dp", "mp"), None),
    )
    return jax.shard_map(
        shards,
        mesh=mesh,
        in_specs=placed,
        out_specs=(P(("dp", "mp"), None), P(("dp", "mp")), P(("dp", "mp"))),
        check_vma=False,
    )
```

```python
import functools

import jax
import jax.numpy as jnp
from jax import lax
from jax.experimental import pallas as pl
from jax.experimental.pallas import tpu as pltpu
from jax.sharding import PartitionSpec as P

R = 256
CAP = 8
LAMBDA = 1.0

MESH = pl.DeviceIdType.MESH
F32 = jnp.float32
BF16 = jnp.bfloat16
NT = (((1,), (1,)), ((), ()))
TN = (((0,), (0,)), ((), ()))
MIB = 1 << 20
PHASES = (0, 40, 80, 112, 128)


def iota(shape, axis):
    return lax.broadcasted_iota(jnp.int32, shape, axis)


def halves(x):
    high = x.astype(BF16)
    return high, (x - high.astype(F32)).astype(BF16)


def thirds(x):
    high, rest = x.astype(BF16), None
    rest = x - high.astype(F32)
    middle = rest.astype(BF16)
    return high, middle, (rest - middle.astype(F32)).astype(BF16)


def one_hot(condition):
    return jnp.where(condition, 1.0, 0.0).astype(BF16)


class Torus:
    def __init__(self):
        dp, self.y = lax.axis_index("dp"), lax.axis_index("mp")
        self.z, self.x, self.core = dp // 8, lax.rem(dp // 2, 4), lax.rem(dp, 2)
        self.zs = [lax.rem(self.z + d, 4) * 8 for d in range(4)]
        self.xs = [lax.rem(self.x + d, 4) * 2 for d in range(4)]
        self.cores = [self.core, 1 - self.core]
        self.ys = [lax.rem(self.y + d, 4) for d in range(4)]

    def peer(self, k):
        digits = 77 * k % 128
        dp = self.zs[digits // 32] + self.xs[digits // 8 % 4] + self.cores[digits // 4 % 2]
        return dp, self.ys[digits % 4]

    def step_of(self, owner):
        dz = lax.rem(owner // 32 + (4 - self.z), 4)
        dx = lax.rem(lax.rem(owner // 8, 4) + (4 - self.x), 4)
        core = lax.rem(lax.rem(owner // 4, 2) + (2 - self.core), 2)
        dy = lax.rem(lax.rem(owner, 4) + (4 - self.y), 4)
        return lax.rem(5 * (dz * 32 + dx * 8 + core * 4 + dy), 128)

    def chip_peer(self, k):
        digits = 29 * k % 64
        dp = self.zs[digits // 16] + self.xs[digits // 4 % 4] + self.core
        return dp, self.ys[digits % 4]

    def sibling(self):
        return self.zs[0] + self.xs[0] + self.cores[1], self.y

    def table_place(self):
        return self.core * 64 + self.z * 16 + self.x * 4 + self.y


def table_place(device):
    return lax.rem(device // 4, 2) * 64 + device // 8 * 4 + lax.rem(device, 4)


def remote(source, target, send_sem, recv_sem, peer):
    return pltpu.make_async_remote_copy(
        src_ref=source,
        dst_ref=target,
        send_sem=send_sem,
        recv_sem=recv_sem,
        device_id=peer,
        device_id_type=MESH,
    )


def row_products(wide, z_ref, slot_ref, out_ref):
    half = [wide[pl.ds(h, 512, stride=2), :].astype(BF16) for h in range(2)]
    coefs = jnp.concatenate(half, axis=1)
    for c in range(8):
        lanes = pl.ds(256 * c, 256)
        product = lax.dot_general(coefs, z_ref[lanes, :], NT, preferred_element_type=F32)
        chosen = iota((512, 256), 0) == slot_ref[:, lanes]
        out_ref[:, lanes] = jnp.sum(jnp.where(chosen, product, 0.0), axis=0, keepdims=True)


def six_left(x, axis=0):
    high, middle, low = thirds(x)
    return jnp.concatenate([high, high, middle, middle, high, low], axis=axis)


def six_right(x, axis=0):
    high, middle, low = thirds(x)
    return jnp.concatenate([high, middle, high, middle, low, high], axis=axis)


def dot6(left, right, dims):
    ((la,), (ra,)), _ = dims
    return lax.dot_general(
        six_left(left, la), six_right(right, ra), dims, preferred_element_type=F32
    )


def factor_packed(packed, pivots, first, between):
    lane = iota((32, 128), 1)
    group = lane // 32 * 32
    local = lane - group
    sub = iota((32, 128), 0)
    local1 = local[0:1]
    roots = jnp.zeros((32, 128), F32)
    for j in range(0, 32, 8):
        below = sub >= j + 8
        columns = [
            jnp.take_along_axis(packed, group + (j + a), axis=1, mode="promise_in_bounds")
            for a in range(8)
        ]
        p = {(a, b): columns[b][j + a:j + a + 1] for a in range(8) for b in range(a, 8)}
        inside = (local1 >= j) & (local1 < j + 8)
        rows = [
            jnp.where(inside, jnp.where(local1 == j + a, 1.0, 0.0), packed[j + a:j + a + 1])
            for a in range(8)
        ]
        change = jnp.zeros((32, 128), F32)
        for a in range(8):
            scale = 1.0 / p[a, a]
            for b in range(a + 1, 8):
                ratio = p[a, b] * scale
                for c in range(b, 8):
                    p[b, c] = p[b, c] - ratio * p[a, c]
                rows[b] = rows[b] - ratio * rows[a]
                columns[b] = columns[b] - columns[a] * ratio
            change = change + columns[a] * (rows[a] * scale)
            pivots[first + j + a:first + j + a + 1, :] = p[a, a]
        kept = jnp.where((local >= j) & (local < j + 8), 0.0, packed) - change
        packed = jnp.where(below, kept, packed)
        for a in range(8):
            packed = jnp.where(sub == j + a, rows[a], packed)
            roots = jnp.where(sub == j + a, lax.rsqrt(p[a, a]), roots)
        between()
        between()
    return jnp.where(local <= sub, packed, 0.0) * roots


def newton(a_ref, grad_ref, likelihood_ref, coef_ref, new_ref, objective_ref, pivots):
    lane = iota((1, 256), 1)
    for m in range(4):
        one_sided = a_ref[m]
        a_ref[m] = 0.5 * (one_sided + one_sided.T)
    blocks = [a_ref[m, 0:32, :] for m in range(4)]
    pending = []

    def between():
        if pending:
            pending.pop(0)()

    for k in range(8):
        low = 32 * k
        packed = jnp.concatenate([b[:, low:low + 32] for b in blocks], axis=1)
        inverse = factor_packed(packed, pivots, low, between)
        while pending:
            between()
        inside = (lane >= low) & (lane < low + 32)
        sign = jnp.where(lane < low, -1.0, 1.0)
        following = []
        for m in range(4):
            own = inverse[:, 32 * m:32 * m + 32]
            wide = jnp.concatenate(
                ([jnp.zeros((32, low), F32)] if low else []) + [own]
                + ([jnp.zeros((32, 224 - low), F32)] if low < 224 else []),
                axis=1,
            )
            half = jnp.where(inside, wide, dot6(own, blocks[m], (((1,), (0,)), ((), ()))))
            left = six_left(half * sign)
            right = six_right(half)
            skipped = [k]
            if k < 7:
                change = lax.dot_general(
                    left[:, low + 32:low + 64], right, TN, preferred_element_type=F32
                )
                ahead = jnp.where(inside, 0.0, a_ref[m, low + 32:low + 64, :]) - change
                following.append(ahead)
                a_ref[m, low + 32:low + 64, :] = ahead
                skipped.append(k + 1)

            def bulk(part, m=m, low=low, own=own, left=left, right=right, inside=inside,
                     skipped=skipped):
                change = lax.dot_general(
                    left[:, 128 * part:128 * part + 128], right, TN, preferred_element_type=F32
                )
                for n in range(4):
                    if 4 * part + n not in skipped:
                        rows = slice(128 * part + 32 * n, 128 * part + 32 * n + 32)
                        a_ref[m, rows, :] = (
                            jnp.where(inside, 0.0, a_ref[m, rows, :]) - change[32 * n:32 * n + 32]
                        )
                if part == 1:
                    a_ref[m, low:low + 32, :] = lax.dot_general(
                        six_left(own), right, TN, preferred_element_type=F32
                    )

            pending += [functools.partial(bulk, part) for part in range(2)]
        blocks = following
    while pending:
        between()
    logs = jnp.sum(jnp.log(pivots[...]), axis=0, keepdims=True)
    side_lane = iota((1, 128), 1)
    news = []
    for m in range(4):
        coef = coef_ref[m:m + 1, :]
        gradient = grad_ref[m] - LAMBDA * coef
        update = dot6(gradient, a_ref[m], (((1,), (0,)), ((), ())))
        new = coef + update[0:1]
        new_ref[m:m + 1, :] = new
        news += [new[:, :128], new[:, 128:]]
        half_logdet = 0.5 * jnp.sum(jnp.where(side_lane == 32 * m, logs, 0.0))
        likelihood = jnp.sum(jnp.where(side_lane == 0, likelihood_ref[m:m + 1, :], 0.0))
        objective_ref[m] = likelihood - 0.5 * LAMBDA * jnp.sum(coef * coef) - half_logdet
    return jnp.concatenate(news, axis=0)


def step_kernel(
    v_hbm, ids_hbm, w_hbm, member_hbm, label_hbm, z_hbm, slots_hbm, coef_hbm,
    new_ref, objective_ref, margin_ref,
    v_ref, ids_ref, w_ref, member_ref, label_ref, z_ref, slots_ref, coef_ref,
    onehot, ids2, part, fixed_part, fixed_recv, fixed_ref, table, wide, target_ref, slot_ref,
    send, recv, side_send, side_recv, a_ref, grad_ref, likelihood_ref, pivots,
    load_sem, table_sem, fixed_sem, side_sem, rows_send_sem, rows_recv_sem,
):
    torus = Torus()

    loads = [
        pltpu.make_async_copy(source, target, load_sem.at[n])
        for n, (source, target) in enumerate((
            (member_hbm, member_ref), (slots_hbm, slots_ref), (z_hbm, z_ref),
            (ids_hbm, ids_ref), (w_hbm, w_ref), (v_hbm, v_ref), (label_hbm, label_ref),
            (coef_hbm, coef_ref),
        ))
    ]
    for load in loads:
        load.start()

    barrier = pltpu.get_barrier_semaphore()
    greeted = iter(range(1, 128))

    def greet(count):
        for _ in range(count):
            k = next(greeted, None)
            if k is not None:
                pl.semaphore_signal(
                    barrier, inc=1, device_id=torus.peer(k), device_id_type=MESH
                )

    greet(47)
    loads[0].wait()
    loads[1].wait()
    for c in range(8):
        lanes = pl.ds(256 * c, 256)
        onehot[:, lanes] = one_hot(iota((512, 256), 0) == member_ref[:, lanes])
        greet(5)
    slots = slots_ref[...]
    sub = iota((8, 512), 0)
    owner = slots // 4
    owner_row = jnp.where(sub == 1, lax.rem(slots, 4), jnp.where(sub == 2, table_place(owner), 0))
    owner_row = jnp.where(sub == 0, torus.step_of(owner), owner_row).astype(F32).astype(BF16)
    before = one_hot(iota((256, 256), 0) < iota((256, 256), 1))
    tally = jnp.concatenate([before, jnp.ones((256, 256), BF16)], axis=1)
    base = jnp.zeros((512, 256), F32)
    for c in range(8):
        lanes = pl.ds(256 * c, 256)
        hot = onehot[:, lanes]
        found = jnp.dot(owner_row, hot, preferred_element_type=F32)
        counted = jnp.dot(hot, tally, preferred_element_type=F32)
        rank = jnp.sum(hot.astype(F32) * (base + counted[:, :256]), axis=0, keepdims=True)
        base = base + counted[:, 256:]
        slot_ref[:, lanes] = (found[2:3] * 4.0 + found[1:2]).astype(jnp.int32)
        target = found[0:1] * 32.0 + found[1:2] * 8.0 + rank
        target_ref[:, lanes] = target.astype(jnp.int32)
        greet(5)

    def pick_rows(c, carry):
        target = target_ref[...] - c * 256
        picked = jnp.zeros((256, 256), F32)
        for piece in range(4):
            lanes = pl.ds(512 * piece, 512)
            hot = one_hot(iota((256, 512), 0) == target[:, 512 * piece:512 * piece + 512])
            picked = picked + jnp.dot(hot, z_ref[lanes, :], preferred_element_type=F32)
        send[pl.ds(c * 8, 8)] = picked.astype(BF16).reshape(8, 32, 256)
        return carry

    def row_copy(places, k, phase):
        return remote(
            send.at[places], recv.at[places], rows_send_sem, rows_recv_sem.at[phase],
            torus.peer(k),
        )

    def pick(low, high):
        lax.fori_loop(low // 8, high // 8, pick_rows, 0)

    def send_rows(low, high, phase):
        for k in range(max(low, 1), high):
            row_copy(k, k, phase).start()

    def send_phase(phase):
        pick(PHASES[phase], PHASES[phase + 1])
        send_rows(PHASES[phase], PHASES[phase + 1], phase)

    for load in loads[3:]:
        load.wait()
    for r in range(64):
        for k in range(2):
            ids2[k, r:r + 1, :] = ids_ref[k:k + 1, 128 * r:128 * r + 128]
    spread = [one_hot(iota((128, 256), 1) == 2 * iota((128, 256), 0) + k) for k in range(2)]
    part[...] = sum(
        jnp.dot(ids2[k].astype(F32).astype(BF16), spread[k], preferred_element_type=F32)
        for k in range(2)
    )
    w2 = jnp.concatenate(halves(w_ref[...]), axis=1)

    def margin_rows(r, carry):
        rows = v_ref[pl.ds(pl.multiple_of(r * 256, 256), 256), :]
        product = lax.dot_general(
            w2, jnp.concatenate([rows, rows], axis=1), NT, preferred_element_type=F32
        )
        chosen = iota((128, 256), 0) == part[pl.ds(r, 1), :].astype(jnp.int32)
        part[pl.ds(r, 1), :] = jnp.sum(jnp.where(chosen, product, 0.0), axis=0, keepdims=True)
        return carry

    lax.fori_loop(0, 64, margin_rows, 0, unroll=4)
    pairs = one_hot(iota((256, 128), 0) // 2 == iota((256, 128), 1))
    fixed_part[...] = sum(
        jnp.dot(piece, pairs, preferred_element_type=F32) for piece in thirds(part[...])
    )

    loads[2].wait()
    pick(0, 16)
    pl.semaphore_wait(barrier, 127)
    for k in range(1, 4):
        remote(
            fixed_part.at[pl.ds(pl.multiple_of(torus.ys[k] * 16, 16), 16)],
            fixed_recv.at[pl.ds(k * 16, 16)],
            fixed_sem.at[0], fixed_sem.at[1],
            (lax.axis_index("dp"), torus.ys[k]),
        ).start()
    send_rows(0, 16, 0)
    pick(16, PHASES[1])
    send_rows(16, PHASES[1], 0)
    recv[0] = send[0]

    waiting = remote(
        fixed_part.at[pl.ds(0, 48)], fixed_recv.at[pl.ds(16, 48)],
        fixed_sem.at[0], fixed_sem.at[1], torus.peer(0),
    )
    waiting.wait_send()
    waiting.wait_recv()
    own = fixed_part[pl.ds(pl.multiple_of(torus.y * 16, 16), 16), :]
    total = own + fixed_recv[16:32] + fixed_recv[32:48] + fixed_recv[48:64]
    for r in range(16):
        fixed_ref[:, 128 * r:128 * r + 128] = total[r:r + 1, :]
    fixed = fixed_ref[...]
    code = label_ref[...].astype(F32) + 1.0
    target = target_ref[...]
    sides = jnp.zeros((128, 128), F32)
    for c in range(4):
        lanes = slice(512 * c, 512 * c + 512)
        step_hot = one_hot(iota((128, 512), 0) == target[:, lanes] // 32)
        within = iota((32, 512), 0) == lax.rem(target[:, lanes], 32)
        values = jnp.concatenate(
            [jnp.where(within, q[:, lanes], 0.0) for q in (fixed, code)]
            + [jnp.zeros((64, 512), F32)],
            axis=0,
        )
        for piece in thirds(values):
            sides = sides + lax.dot_general(step_hot, piece, NT, preferred_element_type=F32)
    for k in range(128):
        side_send[k] = sides[k:k + 1, :]

    def side_copy(places, k):
        return remote(
            side_send.at[places], side_recv.at[places], side_sem.at[0], side_sem.at[1],
            torus.peer(k),
        )

    for k in range(1, 128):
        side_copy(k, k).start()
    side_recv[0] = side_send[0]

    for phase in (1, 2, 3):
        send_phase(phase)

    waiting = side_copy(pl.ds(0, 127), 0)
    waiting.wait_send()
    waiting.wait_recv()
    eye = jnp.where(iota((256, 256), 0) == iota((256, 256), 1), LAMBDA, 0.0)
    ones = jnp.ones((256, 128), BF16)
    for phase in range(4):
        low, high = PHASES[phase], PHASES[phase + 1]
        count = high - low
        row_copy(pl.ds(0, count - (phase == 0)), 0, phase).wait_recv()
        lane = iota((count, 8, 128), 2) - iota((count, 8, 128), 1)
        sides = jnp.broadcast_to(side_recv[low:high], (count, 8, 128))
        for m in range(4):
            rows = recv[low:high, 8 * m:8 * m + 8, :].astype(F32).reshape(8 * count, 256)
            rows_b = rows.astype(BF16)
            coef_b = jnp.broadcast_to(coef_ref[m:m + 1, :], (128, 256)).astype(BF16)
            known = jnp.where(lane == 8 * m, sides, 0.0).reshape(8 * count, 128)
            known = jnp.concatenate(halves(known), axis=1)
            score = lax.dot_general(rows_b, coef_b, NT, preferred_element_type=F32)
            score = score + jnp.dot(known, ones, preferred_element_type=F32)
            code = jnp.where(lane == 32 + 8 * m, sides, 0.0).reshape(8 * count, 128)
            code = jnp.dot(code.astype(BF16), ones[:128], preferred_element_type=F32)
            live = code > 0.5
            label = code - 1.0
            small = jnp.exp(-jnp.abs(score))
            inverse = 1.0 / (1.0 + small)
            probability = jnp.where(score >= 0.0, 1.0, small) * inverse
            weight = jnp.where(live, small * inverse * inverse, 0.0)
            residual = jnp.where(live, label - probability, 0.0).astype(BF16)
            gain = label * score - (jnp.maximum(score, 0.0) + jnp.log1p(small))
            gain = jnp.sum(jnp.where(live, gain, 0.0), axis=0, keepdims=True)
            weighted = (jnp.concatenate([weight, weight], axis=1) * rows).astype(BF16)
            update = lax.dot_general(weighted, rows_b, TN, preferred_element_type=F32)
            pull = lax.dot_general(residual, rows_b, TN, preferred_element_type=F32)[0:8]
            if phase == 0:
                a_ref[m] = eye + update
                grad_ref[m] = pull
                likelihood_ref[m:m + 1, :] = gain
            else:
                a_ref[m] += update
                grad_ref[m] += pull
                likelihood_ref[m:m + 1, :] += gain

    block = newton(a_ref, grad_ref, likelihood_ref, coef_ref, new_ref, objective_ref, pivots)
    row_copy(pl.ds(0, 127), 0, 0).wait_send()

    at = torus.table_place()
    table[pl.ds(at, 1)] = block.astype(BF16).reshape(1, 8, 128)

    def table_copy(blocks, number, peer):
        return remote(
            table.at[blocks], table.at[blocks], table_sem.at[number], table_sem.at[2 + number],
            peer,
        )

    for k in range(1, 64):
        table_copy(pl.ds(at, 1), 0, torus.chip_peer(k)).start()
    waiting = table_copy(pl.ds(0, 63), 0, torus.sibling())
    waiting.wait_send()
    waiting.wait_recv()
    swap = table_copy(pl.ds(torus.core * 64, 64), 1, torus.sibling())
    swap.start()
    swap.wait_send()
    swap.wait_recv()
    wide[...] = table[...].astype(F32).reshape(1024, 128)
    row_products(wide, z_ref, slot_ref, margin_ref)
    margin_ref[...] += fixed_ref[...]


def step(v, ids, fixed_coef, member, labels, z, slots, coef):
    vmem = pl.BlockSpec(memory_space=pltpu.VMEM)
    operands = (v, ids, fixed_coef, member, labels, z, slots, coef)
    return pl.pallas_call(
        step_kernel,
        out_shape=(
            jax.ShapeDtypeStruct((4, 256), F32),
            jax.ShapeDtypeStruct((4,), F32),
            jax.ShapeDtypeStruct((1, 2048), F32),
        ),
        in_specs=[pl.BlockSpec(memory_space=pl.ANY)] * 8,
        out_specs=(vmem, pl.BlockSpec(memory_space=pltpu.SMEM), vmem),
        scratch_shapes=[pltpu.VMEM(x.shape, x.dtype) for x in operands] + [
            pltpu.VMEM((512, 2048), BF16),
            pltpu.VMEM((2, 64, 128), jnp.int32),
            pltpu.VMEM((64, 256), F32),
            pltpu.VMEM((64, 128), F32),
            pltpu.VMEM((64, 128), F32),
            pltpu.VMEM((1, 2048), F32),
            pltpu.VMEM((128, 8, 128), BF16),
            pltpu.VMEM((1024, 128), F32),
            pltpu.VMEM((1, 2048), jnp.int32),
            pltpu.VMEM((1, 2048), jnp.int32),
            pltpu.VMEM((128, 32, 256), BF16),
            pltpu.VMEM((128, 32, 256), BF16),
            pltpu.VMEM((128, 1, 128), F32),
            pltpu.VMEM((128, 1, 128), F32),
            pltpu.VMEM((4, 256, 256), F32),
            pltpu.VMEM((4, 8, 256), F32),
            pltpu.VMEM((4, 128), F32),
            pltpu.VMEM((256, 128), F32),
            pltpu.SemaphoreType.DMA((8,)),
            pltpu.SemaphoreType.DMA((4,)),
            pltpu.SemaphoreType.DMA((2,)),
            pltpu.SemaphoreType.DMA((2,)),
            pltpu.SemaphoreType.DMA,
            pltpu.SemaphoreType.DMA((4,)),
        ],
        compiler_params=pltpu.CompilerParams(
            collective_id=0, has_side_effects=True, vmem_limit_bytes=56 * MIB
        ),
        name="step",
    )(*operands)


def hand_over_kernel(*refs):
    count = (len(refs) - 1) // 2
    copies = [
        pltpu.make_async_copy(refs[n], refs[count + n], refs[-1].at[n]) for n in range(count)
    ]
    for copy in copies:
        copy.start()
    for copy in copies:
        copy.wait()


def hand_over(*arrays):
    anywhere = pl.BlockSpec(memory_space=pl.ANY)
    return pl.pallas_call(
        hand_over_kernel,
        out_shape=tuple(jax.ShapeDtypeStruct(x.shape, x.dtype) for x in arrays),
        in_specs=[anywhere] * len(arrays),
        out_specs=(anywhere,) * len(arrays),
        scratch_shapes=[pltpu.SemaphoreType.DMA((len(arrays),))],
        name="hand_over",
    )(*arrays)


def shards(feat_values, feat_blocks, fixed_coef, member_of, labels, re_features, member_slot, coef):
    new_coef, objective, margin = step(
        feat_values.reshape(16384, 128),
        feat_blocks.T,
        fixed_coef,
        member_of.reshape(1, 2048),
        labels.reshape(1, 2048),
        re_features,
        member_slot.reshape(1, 512),
        coef,
    )
    new_coef, objective, margin = hand_over(new_coef, objective, margin)
    return (new_coef, objective, margin.reshape(2048))


def solution(mesh):
    placed = (
        P("dp", "mp", None),
        P("dp", "mp"),
        P(),
        P(("dp", "mp"), None),
        P(("dp", "mp")),
        P(("dp", "mp"), None),
        P(),
        P(("dp", "mp"), None),
    )
    return jax.shard_map(
        shards,
        mesh=mesh,
        in_specs=placed,
        out_specs=(P(("dp", "mp"), None), P(("dp", "mp")), P(("dp", "mp"))),
        check_vma=False,
    )
```

```python
import functools

import jax
import jax.numpy as jnp
from jax import lax
from jax.experimental import pallas as pl
from jax.experimental.pallas import tpu as pltpu
from jax.sharding import PartitionSpec as P

R = 256
CAP = 8
LAMBDA = 1.0

MESH = pl.DeviceIdType.MESH
F32 = jnp.float32
BF16 = jnp.bfloat16
NT = (((1,), (1,)), ((), ()))
TN = (((0,), (0,)), ((), ()))
MIB = 1 << 20
PHASES = (0, 40, 80, 112, 128)


def iota(shape, axis):
    return lax.broadcasted_iota(jnp.int32, shape, axis)


def halves(x):
    high = x.astype(BF16)
    return high, (x - high.astype(F32)).astype(BF16)


def thirds(x):
    high, rest = x.astype(BF16), None
    rest = x - high.astype(F32)
    middle = rest.astype(BF16)
    return high, middle, (rest - middle.astype(F32)).astype(BF16)


def one_hot(condition):
    return jnp.where(condition, 1.0, 0.0).astype(BF16)


class Torus:
    def __init__(self):
        dp, self.y = lax.axis_index("dp"), lax.axis_index("mp")
        self.z, self.x, self.core = dp // 8, lax.rem(dp // 2, 4), lax.rem(dp, 2)
        self.zs = [lax.rem(self.z + d, 4) * 8 for d in range(4)]
        self.xs = [lax.rem(self.x + d, 4) * 2 for d in range(4)]
        self.cores = [self.core, 1 - self.core]
        self.ys = [lax.rem(self.y + d, 4) for d in range(4)]

    def peer(self, k):
        digits = 77 * k % 128
        dp = self.zs[digits // 32] + self.xs[digits // 8 % 4] + self.cores[digits // 4 % 2]
        return dp, self.ys[digits % 4]

    def step_of(self, owner):
        dz = lax.rem(owner // 32 + (4 - self.z), 4)
        dx = lax.rem(lax.rem(owner // 8, 4) + (4 - self.x), 4)
        core = lax.rem(lax.rem(owner // 4, 2) + (2 - self.core), 2)
        dy = lax.rem(lax.rem(owner, 4) + (4 - self.y), 4)
        return lax.rem(5 * (dz * 32 + dx * 8 + core * 4 + dy), 128)

    def chip_peer(self, k):
        digits = 29 * k % 64
        dp = self.zs[digits // 16] + self.xs[digits // 4 % 4] + self.core
        return dp, self.ys[digits % 4]

    def sibling(self):
        return self.zs[0] + self.xs[0] + self.cores[1], self.y

    def table_place(self):
        return self.core * 64 + self.z * 16 + self.x * 4 + self.y


def table_place(device):
    return lax.rem(device // 4, 2) * 64 + device // 8 * 4 + lax.rem(device, 4)


def remote(source, target, send_sem, recv_sem, peer):
    return pltpu.make_async_remote_copy(
        src_ref=source,
        dst_ref=target,
        send_sem=send_sem,
        recv_sem=recv_sem,
        device_id=peer,
        device_id_type=MESH,
    )


def add_row_products(wide, first, z_ref, slot_ref, out_ref):
    half = [wide[pl.ds(first * 2 + h, 256, stride=2), :].astype(BF16) for h in range(2)]
    coefs = jnp.concatenate(half, axis=1)
    for c in range(8):
        lanes = pl.ds(256 * c, 256)
        product = lax.dot_general(coefs, z_ref[lanes, :], NT, preferred_element_type=F32)
        chosen = iota((256, 256), 0) == slot_ref[:, lanes] - first
        out_ref[:, lanes] += jnp.sum(jnp.where(chosen, product, 0.0), axis=0, keepdims=True)


def six_left(x, axis=0):
    high, middle, low = thirds(x)
    return jnp.concatenate([high, high, middle, middle, high, low], axis=axis)


def six_right(x, axis=0):
    high, middle, low = thirds(x)
    return jnp.concatenate([high, middle, high, middle, low, high], axis=axis)


def dot6(left, right, dims):
    ((la,), (ra,)), _ = dims
    return lax.dot_general(
        six_left(left, la), six_right(right, ra), dims, preferred_element_type=F32
    )


def factor_packed(packed, pivots, first, between):
    lane = iota((32, 128), 1)
    group = lane // 32 * 32
    local = lane - group
    sub = iota((32, 128), 0)
    local1 = local[0:1]
    roots = jnp.zeros((32, 128), F32)
    for j in range(0, 32, 8):
        below = sub >= j + 8
        columns = [
            jnp.take_along_axis(packed, group + (j + a), axis=1, mode="promise_in_bounds")
            for a in range(8)
        ]
        p = {(a, b): columns[b][j + a:j + a + 1] for a in range(8) for b in range(a, 8)}
        inside = (local1 >= j) & (local1 < j + 8)
        rows = [
            jnp.where(inside, jnp.where(local1 == j + a, 1.0, 0.0), packed[j + a:j + a + 1])
            for a in range(8)
        ]
        change = jnp.zeros((32, 128), F32)
        for a in range(8):
            scale = 1.0 / p[a, a]
            for b in range(a + 1, 8):
                ratio = p[a, b] * scale
                for c in range(b, 8):
                    p[b, c] = p[b, c] - ratio * p[a, c]
                rows[b] = rows[b] - ratio * rows[a]
                columns[b] = columns[b] - columns[a] * ratio
            change = change + columns[a] * (rows[a] * scale)
            pivots[first + j + a:first + j + a + 1, :] = p[a, a]
        kept = jnp.where((local >= j) & (local < j + 8), 0.0, packed) - change
        packed = jnp.where(below, kept, packed)
        for a in range(8):
            packed = jnp.where(sub == j + a, rows[a], packed)
            roots = jnp.where(sub == j + a, lax.rsqrt(p[a, a]), roots)
        between()
        between()
    return jnp.where(local <= sub, packed, 0.0) * roots


def newton(a_ref, grad_ref, likelihood_ref, coef_ref, new_ref, objective_ref, pivots):
    lane = iota((1, 256), 1)
    for m in range(4):
        one_sided = a_ref[m]
        a_ref[m] = 0.5 * (one_sided + one_sided.T)
    blocks = [a_ref[m, 0:32, :] for m in range(4)]
    pending = []

    def between():
        if pending:
            pending.pop(0)()

    for k in range(8):
        low = 32 * k
        packed = jnp.concatenate([b[:, low:low + 32] for b in blocks], axis=1)
        inverse = factor_packed(packed, pivots, low, between)
        while pending:
            between()
        inside = (lane >= low) & (lane < low + 32)
        sign = jnp.where(lane < low, -1.0, 1.0)
        following = []
        for m in range(4):
            own = inverse[:, 32 * m:32 * m + 32]
            wide = jnp.concatenate(
                ([jnp.zeros((32, low), F32)] if low else []) + [own]
                + ([jnp.zeros((32, 224 - low), F32)] if low < 224 else []),
                axis=1,
            )
            half = jnp.where(inside, wide, dot6(own, blocks[m], (((1,), (0,)), ((), ()))))
            left = six_left(half * sign)
            right = six_right(half)
            skipped = [k]
            if k < 7:
                change = lax.dot_general(
                    left[:, low + 32:low + 64], right, TN, preferred_element_type=F32
                )
                ahead = jnp.where(inside, 0.0, a_ref[m, low + 32:low + 64, :]) - change
                following.append(ahead)
                a_ref[m, low + 32:low + 64, :] = ahead
                skipped.append(k + 1)

            def bulk(part, m=m, low=low, own=own, left=left, right=right, inside=inside,
                     skipped=skipped):
                change = lax.dot_general(
                    left[:, 128 * part:128 * part + 128], right, TN, preferred_element_type=F32
                )
                for n in range(4):
                    if 4 * part + n not in skipped:
                        rows = slice(128 * part + 32 * n, 128 * part + 32 * n + 32)
                        a_ref[m, rows, :] = (
                            jnp.where(inside, 0.0, a_ref[m, rows, :]) - change[32 * n:32 * n + 32]
                        )
                if part == 1:
                    a_ref[m, low:low + 32, :] = lax.dot_general(
                        six_left(own), right, TN, preferred_element_type=F32
                    )

            pending += [functools.partial(bulk, part) for part in range(2)]
        blocks = following
    while pending:
        between()
    logs = jnp.sum(jnp.log(pivots[...]), axis=0, keepdims=True)
    side_lane = iota((1, 128), 1)
    news = []
    for m in range(4):
        coef = coef_ref[m:m + 1, :]
        gradient = grad_ref[m] - LAMBDA * coef
        update = dot6(gradient, a_ref[m], (((1,), (0,)), ((), ())))
        new = coef + update[0:1]
        new_ref[m:m + 1, :] = new
        news += [new[:, :128], new[:, 128:]]
        half_logdet = 0.5 * jnp.sum(jnp.where(side_lane == 32 * m, logs, 0.0))
        likelihood = jnp.sum(jnp.where(side_lane == 0, likelihood_ref[m:m + 1, :], 0.0))
        objective_ref[m] = likelihood - 0.5 * LAMBDA * jnp.sum(coef * coef) - half_logdet
    return jnp.concatenate(news, axis=0)


def step_kernel(
    v_hbm, ids_hbm, w_hbm, member_hbm, label_hbm, z_hbm, slots_hbm, coef_hbm,
    new_ref, objective_ref, margin_ref,
    v_ref, ids_ref, w_ref, member_ref, label_ref, z_ref, slots_ref, coef_ref,
    onehot, ids2, part, fixed_part, fixed_recv, fixed_ref, table, wide, target_ref, slot_ref,
    send, recv, side_send, side_recv, a_ref, grad_ref, likelihood_ref, pivots,
    load_sem, table_sem, fixed_sem, side_sem, rows_send_sem, rows_recv_sem,
):
    torus = Torus()

    loads = [
        pltpu.make_async_copy(source, target, load_sem.at[n])
        for n, (source, target) in enumerate((
            (member_hbm, member_ref), (slots_hbm, slots_ref), (z_hbm, z_ref),
            (ids_hbm, ids_ref), (w_hbm, w_ref), (v_hbm, v_ref), (label_hbm, label_ref),
            (coef_hbm, coef_ref),
        ))
    ]
    for load in loads:
        load.start()

    barrier = pltpu.get_barrier_semaphore()
    greeted = iter(range(1, 128))

    def greet(count):
        for _ in range(count):
            k = next(greeted, None)
            if k is not None:
                pl.semaphore_signal(
                    barrier, inc=1, device_id=torus.peer(k), device_id_type=MESH
                )

    greet(127)
    loads[0].wait()
    loads[1].wait()
    for c in range(8):
        lanes = pl.ds(256 * c, 256)
        onehot[:, lanes] = one_hot(iota((512, 256), 0) == member_ref[:, lanes])
        greet(5)
    slots = slots_ref[...]
    sub = iota((8, 512), 0)
    owner = slots // 4
    owner_row = jnp.where(sub == 1, lax.rem(slots, 4), jnp.where(sub == 2, table_place(owner), 0))
    owner_row = jnp.where(sub == 0, torus.step_of(owner), owner_row).astype(F32).astype(BF16)
    before = one_hot(iota((256, 256), 0) < iota((256, 256), 1))
    tally = jnp.concatenate([before, jnp.ones((256, 256), BF16)], axis=1)
    base = jnp.zeros((512, 256), F32)
    for c in range(8):
        lanes = pl.ds(256 * c, 256)
        hot = onehot[:, lanes]
        found = jnp.dot(owner_row, hot, preferred_element_type=F32)
        counted = jnp.dot(hot, tally, preferred_element_type=F32)
        rank = jnp.sum(hot.astype(F32) * (base + counted[:, :256]), axis=0, keepdims=True)
        base = base + counted[:, 256:]
        slot_ref[:, lanes] = (found[2:3] * 4.0 + found[1:2]).astype(jnp.int32)
        target = found[0:1] * 32.0 + found[1:2] * 8.0 + rank
        target_ref[:, lanes] = target.astype(jnp.int32)
        greet(5)

    def pick_rows(c, carry):
        target = target_ref[...] - c * 256
        picked = jnp.zeros((256, 256), F32)
        for piece in range(4):
            lanes = pl.ds(512 * piece, 512)
            hot = one_hot(iota((256, 512), 0) == target[:, 512 * piece:512 * piece + 512])
            picked = picked + jnp.dot(hot, z_ref[lanes, :], preferred_element_type=F32)
        send[pl.ds(c * 8, 8)] = picked.astype(BF16).reshape(8, 32, 256)
        return carry

    def row_copy(places, k, phase):
        return remote(
            send.at[places], recv.at[places], rows_send_sem, rows_recv_sem.at[phase],
            torus.peer(k),
        )

    def pick(low, high):
        lax.fori_loop(low // 8, high // 8, pick_rows, 0)

    def send_rows(low, high, phase):
        for k in range(max(low, 1), high):
            row_copy(k, k, phase).start()

    def send_phase(phase):
        pick(PHASES[phase], PHASES[phase + 1])
        send_rows(PHASES[phase], PHASES[phase + 1], phase)

    for load in loads[3:]:
        load.wait()
    for r in range(64):
        for k in range(2):
            ids2[k, r:r + 1, :] = ids_ref[k:k + 1, 128 * r:128 * r + 128]
    spread = [one_hot(iota((128, 256), 1) == 2 * iota((128, 256), 0) + k) for k in range(2)]
    part[...] = sum(
        jnp.dot(ids2[k].astype(F32).astype(BF16), spread[k], preferred_element_type=F32)
        for k in range(2)
    )
    w2 = jnp.concatenate(halves(w_ref[...]), axis=1)

    def margin_rows(r, carry):
        rows = v_ref[pl.ds(pl.multiple_of(r * 256, 256), 256), :]
        product = lax.dot_general(
            w2, jnp.concatenate([rows, rows], axis=1), NT, preferred_element_type=F32
        )
        chosen = iota((128, 256), 0) == part[pl.ds(r, 1), :].astype(jnp.int32)
        part[pl.ds(r, 1), :] = jnp.sum(jnp.where(chosen, product, 0.0), axis=0, keepdims=True)
        return carry

    lax.fori_loop(0, 64, margin_rows, 0, unroll=4)
    pairs = one_hot(iota((256, 128), 0) // 2 == iota((256, 128), 1))
    fixed_part[...] = sum(
        jnp.dot(piece, pairs, preferred_element_type=F32) for piece in thirds(part[...])
    )

    loads[2].wait()
    pick(0, 16)
    pl.semaphore_wait(barrier, 127)
    for k in range(1, 4):
        remote(
            fixed_part.at[pl.ds(pl.multiple_of(torus.ys[k] * 16, 16), 16)],
            fixed_recv.at[pl.ds(k * 16, 16)],
            fixed_sem.at[0], fixed_sem.at[1],
            (lax.axis_index("dp"), torus.ys[k]),
        ).start()
    send_rows(0, 16, 0)
    pick(16, PHASES[1])
    send_rows(16, PHASES[1], 0)
    recv[0] = send[0]

    waiting = remote(
        fixed_part.at[pl.ds(0, 48)], fixed_recv.at[pl.ds(16, 48)],
        fixed_sem.at[0], fixed_sem.at[1], torus.peer(0),
    )
    waiting.wait_send()
    waiting.wait_recv()
    own = fixed_part[pl.ds(pl.multiple_of(torus.y * 16, 16), 16), :]
    total = own + fixed_recv[16:32] + fixed_recv[32:48] + fixed_recv[48:64]
    for r in range(16):
        fixed_ref[:, 128 * r:128 * r + 128] = total[r:r + 1, :]
    fixed = fixed_ref[...]
    code = label_ref[...].astype(F32) + 1.0
    target = target_ref[...]
    sides = jnp.zeros((128, 128), F32)
    for c in range(4):
        lanes = slice(512 * c, 512 * c + 512)
        step_hot = one_hot(iota((128, 512), 0) == target[:, lanes] // 32)
        within = iota((32, 512), 0) == lax.rem(target[:, lanes], 32)
        values = jnp.concatenate(
            [jnp.where(within, q[:, lanes], 0.0) for q in (fixed, code)]
            + [jnp.zeros((64, 512), F32)],
            axis=0,
        )
        for piece in thirds(values):
            sides = sides + lax.dot_general(step_hot, piece, NT, preferred_element_type=F32)
    for k in range(128):
        side_send[k] = sides[k:k + 1, :]

    def side_copy(places, k):
        return remote(
            side_send.at[places], side_recv.at[places], side_sem.at[0], side_sem.at[1],
            torus.peer(k),
        )

    for k in range(1, 128):
        side_copy(k, k).start()
    side_recv[0] = side_send[0]

    for phase in range(1, len(PHASES) - 1):
        send_phase(phase)

    waiting = side_copy(pl.ds(0, 127), 0)
    waiting.wait_send()
    waiting.wait_recv()
    eye = jnp.where(iota((256, 256), 0) == iota((256, 256), 1), LAMBDA, 0.0)
    ones = jnp.ones((256, 128), BF16)
    for phase in range(len(PHASES) - 1):
        low, high = PHASES[phase], PHASES[phase + 1]
        count = high - low
        row_copy(pl.ds(0, count - (phase == 0)), 0, phase).wait_recv()
        lane = iota((count, 8, 128), 2) - iota((count, 8, 128), 1)
        sides = jnp.broadcast_to(side_recv[low:high], (count, 8, 128))
        for m in range(4):
            rows = recv[low:high, 8 * m:8 * m + 8, :].astype(F32).reshape(8 * count, 256)
            rows_b = rows.astype(BF16)
            coef_b = jnp.broadcast_to(coef_ref[m:m + 1, :], (128, 256)).astype(BF16)
            known = jnp.where(lane == 8 * m, sides, 0.0).reshape(8 * count, 128)
            known = jnp.concatenate(halves(known), axis=1)
            score = lax.dot_general(rows_b, coef_b, NT, preferred_element_type=F32)
            score = score + jnp.dot(known, ones, preferred_element_type=F32)
            code = jnp.where(lane == 32 + 8 * m, sides, 0.0).reshape(8 * count, 128)
            code = jnp.dot(code.astype(BF16), ones[:128], preferred_element_type=F32)
            live = code > 0.5
            label = code - 1.0
            small = jnp.exp(-jnp.abs(score))
            inverse = 1.0 / (1.0 + small)
            probability = jnp.where(score >= 0.0, 1.0, small) * inverse
            weight = jnp.where(live, small * inverse * inverse, 0.0)
            residual = jnp.where(live, label - probability, 0.0).astype(BF16)
            gain = label * score - (jnp.maximum(score, 0.0) + jnp.log1p(small))
            gain = jnp.sum(jnp.where(live, gain, 0.0), axis=0, keepdims=True)
            weighted = (jnp.concatenate([weight, weight], axis=1) * rows).astype(BF16)
            update = lax.dot_general(weighted, rows_b, TN, preferred_element_type=F32)
            pull = lax.dot_general(residual, rows_b, TN, preferred_element_type=F32)[0:8]
            if phase == 0:
                a_ref[m] = eye + update
                grad_ref[m] = pull
                likelihood_ref[m:m + 1, :] = gain
            else:
                a_ref[m] += update
                grad_ref[m] += pull
                likelihood_ref[m:m + 1, :] += gain

    block = newton(a_ref, grad_ref, likelihood_ref, coef_ref, new_ref, objective_ref, pivots)
    row_copy(pl.ds(0, 127), 0, 0).wait_send()

    at = torus.table_place()
    table[pl.ds(at, 1)] = block.astype(BF16).reshape(1, 8, 128)

    def table_copy(blocks, number, peer):
        return remote(
            table.at[blocks], table.at[blocks], table_sem.at[number], table_sem.at[2 + number],
            peer,
        )

    for k in range(1, 64):
        table_copy(pl.ds(at, 1), 0, torus.chip_peer(k)).start()
    waiting = table_copy(pl.ds(0, 63), 0, torus.sibling())
    waiting.wait_send()
    waiting.wait_recv()
    swap = table_copy(pl.ds(torus.core * 64, 64), 1, torus.sibling())
    swap.start()
    margin_ref[...] = fixed_ref[...]

    def add_margins(core):
        here = pl.ds(core * 64, 64)
        rows = pl.ds(pl.multiple_of(core * 512, 512), 512)
        wide[rows, :] = table[here].astype(F32).reshape(512, 128)
        add_row_products(wide, core * 256, z_ref, slot_ref, margin_ref)

    add_margins(torus.core)
    swap.wait_send()
    swap.wait_recv()
    add_margins(torus.cores[1])


def step(v, ids, fixed_coef, member, labels, z, slots, coef):
    vmem = pl.BlockSpec(memory_space=pltpu.VMEM)
    operands = (v, ids, fixed_coef, member, labels, z, slots, coef)
    return pl.pallas_call(
        step_kernel,
        out_shape=(
            jax.ShapeDtypeStruct((4, 256), F32),
            jax.ShapeDtypeStruct((4,), F32),
            jax.ShapeDtypeStruct((1, 2048), F32),
        ),
        in_specs=[pl.BlockSpec(memory_space=pl.ANY)] * 8,
        out_specs=(vmem, pl.BlockSpec(memory_space=pltpu.SMEM), vmem),
        scratch_shapes=[pltpu.VMEM(x.shape, x.dtype) for x in operands] + [
            pltpu.VMEM((512, 2048), BF16),
            pltpu.VMEM((2, 64, 128), jnp.int32),
            pltpu.VMEM((64, 256), F32),
            pltpu.VMEM((64, 128), F32),
            pltpu.VMEM((64, 128), F32),
            pltpu.VMEM((1, 2048), F32),
            pltpu.VMEM((128, 8, 128), BF16),
            pltpu.VMEM((1024, 128), F32),
            pltpu.VMEM((1, 2048), jnp.int32),
            pltpu.VMEM((1, 2048), jnp.int32),
            pltpu.VMEM((128, 32, 256), BF16),
            pltpu.VMEM((128, 32, 256), BF16),
            pltpu.VMEM((128, 1, 128), F32),
            pltpu.VMEM((128, 1, 128), F32),
            pltpu.VMEM((4, 256, 256), F32),
            pltpu.VMEM((4, 8, 256), F32),
            pltpu.VMEM((4, 128), F32),
            pltpu.VMEM((256, 128), F32),
            pltpu.SemaphoreType.DMA((8,)),
            pltpu.SemaphoreType.DMA((4,)),
            pltpu.SemaphoreType.DMA((2,)),
            pltpu.SemaphoreType.DMA((2,)),
            pltpu.SemaphoreType.DMA,
            pltpu.SemaphoreType.DMA((len(PHASES) - 1,)),
        ],
        compiler_params=pltpu.CompilerParams(
            collective_id=0, has_side_effects=True, vmem_limit_bytes=56 * MIB
        ),
        name="step",
    )(*operands)


def hand_over_kernel(*refs):
    count = (len(refs) - 1) // 2
    copies = [
        pltpu.make_async_copy(refs[n], refs[count + n], refs[-1].at[n]) for n in range(count)
    ]
    for copy in copies:
        copy.start()
    for copy in copies:
        copy.wait()


def hand_over(*arrays):
    anywhere = pl.BlockSpec(memory_space=pl.ANY)
    return pl.pallas_call(
        hand_over_kernel,
        out_shape=tuple(jax.ShapeDtypeStruct(x.shape, x.dtype) for x in arrays),
        in_specs=[anywhere] * len(arrays),
        out_specs=(anywhere,) * len(arrays),
        scratch_shapes=[pltpu.SemaphoreType.DMA((len(arrays),))],
        name="hand_over",
    )(*arrays)


def shards(feat_values, feat_blocks, fixed_coef, member_of, labels, re_features, member_slot, coef):
    new_coef, objective, margin = step(
        feat_values.reshape(16384, 128),
        feat_blocks.T,
        fixed_coef,
        member_of.reshape(1, 2048),
        labels.reshape(1, 2048),
        re_features,
        member_slot.reshape(1, 512),
        coef,
    )
    new_coef, objective, margin = hand_over(new_coef, objective, margin)
    return (new_coef, objective, margin.reshape(2048))


def solution(mesh):
    placed = (
        P("dp", "mp", None),
        P("dp", "mp"),
        P(),
        P(("dp", "mp"), None),
        P(("dp", "mp")),
        P(("dp", "mp"), None),
        P(),
        P(("dp", "mp"), None),
    )
    return jax.shard_map(
        shards,
        mesh=mesh,
        in_specs=placed,
        out_specs=(P(("dp", "mp"), None), P(("dp", "mp")), P(("dp", "mp"))),
        check_vma=False,
    )
```

```python
import functools

import jax
import jax.numpy as jnp
from jax import lax
from jax.experimental import pallas as pl
from jax.experimental.pallas import tpu as pltpu
from jax.sharding import PartitionSpec as P

R = 256
CAP = 8
LAMBDA = 1.0

MESH = pl.DeviceIdType.MESH
F32 = jnp.float32
BF16 = jnp.bfloat16
NT = (((1,), (1,)), ((), ()))
TN = (((0,), (0,)), ((), ()))
MIB = 1 << 20
PHASES = (0, 40, 80, 112, 128)


def iota(shape, axis):
    return lax.broadcasted_iota(jnp.int32, shape, axis)


def halves(x):
    high = x.astype(BF16)
    return high, (x - high.astype(F32)).astype(BF16)


def thirds(x):
    high, rest = x.astype(BF16), None
    rest = x - high.astype(F32)
    middle = rest.astype(BF16)
    return high, middle, (rest - middle.astype(F32)).astype(BF16)


def one_hot(condition):
    return jnp.where(condition, 1.0, 0.0).astype(BF16)


class Torus:
    def __init__(self):
        dp, self.y = lax.axis_index("dp"), lax.axis_index("mp")
        self.z, self.x, self.core = dp // 8, lax.rem(dp // 2, 4), lax.rem(dp, 2)
        self.zs = [lax.rem(self.z + d, 4) * 8 for d in range(4)]
        self.xs = [lax.rem(self.x + d, 4) * 2 for d in range(4)]
        self.cores = [self.core, 1 - self.core]
        self.ys = [lax.rem(self.y + d, 4) for d in range(4)]

    def peer(self, k):
        digits = 77 * k % 128
        dp = self.zs[digits // 32] + self.xs[digits // 8 % 4] + self.cores[digits // 4 % 2]
        return dp, self.ys[digits % 4]

    def step_of(self, owner):
        dz = lax.rem(owner // 32 + (4 - self.z), 4)
        dx = lax.rem(lax.rem(owner // 8, 4) + (4 - self.x), 4)
        core = lax.rem(lax.rem(owner // 4, 2) + (2 - self.core), 2)
        dy = lax.rem(lax.rem(owner, 4) + (4 - self.y), 4)
        return lax.rem(5 * (dz * 32 + dx * 8 + core * 4 + dy), 128)

    def chip_peer(self, k):
        digits = 29 * k % 64
        dp = self.zs[digits // 16] + self.xs[digits // 4 % 4] + self.core
        return dp, self.ys[digits % 4]

    def sibling(self):
        return self.zs[0] + self.xs[0] + self.cores[1], self.y

    def table_place(self):
        return self.core * 64 + self.z * 16 + self.x * 4 + self.y


def table_place(device):
    return lax.rem(device // 4, 2) * 64 + device // 8 * 4 + lax.rem(device, 4)


def remote(source, target, send_sem, recv_sem, peer):
    return pltpu.make_async_remote_copy(
        src_ref=source,
        dst_ref=target,
        send_sem=send_sem,
        recv_sem=recv_sem,
        device_id=peer,
        device_id_type=MESH,
    )


def add_row_products(wide, first, z_ref, slot_ref, out_ref):
    half = [wide[pl.ds(first * 2 + h, 256, stride=2), :].astype(BF16) for h in range(2)]
    coefs = jnp.concatenate(half, axis=1)
    for c in range(8):
        lanes = pl.ds(256 * c, 256)
        product = lax.dot_general(coefs, z_ref[lanes, :], NT, preferred_element_type=F32)
        chosen = iota((256, 256), 0) == slot_ref[:, lanes] - first
        out_ref[:, lanes] += jnp.sum(jnp.where(chosen, product, 0.0), axis=0, keepdims=True)


def six_left(x, axis=0):
    high, middle, low = thirds(x)
    return jnp.concatenate([high, high, middle, middle, high, low], axis=axis)


def six_right(x, axis=0):
    high, middle, low = thirds(x)
    return jnp.concatenate([high, middle, high, middle, low, high], axis=axis)


def dot6(left, right, dims):
    ((la,), (ra,)), _ = dims
    return lax.dot_general(
        six_left(left, la), six_right(right, ra), dims, preferred_element_type=F32
    )


def factor_packed(packed, pivots, first, between):
    lane = iota((32, 128), 1)
    group = lane // 32 * 32
    local = lane - group
    sub = iota((32, 128), 0)
    local1 = local[0:1]
    roots = jnp.zeros((32, 128), F32)
    for j in range(0, 32, 8):
        below = sub >= j + 8
        columns = [
            jnp.take_along_axis(packed, group + (j + a), axis=1, mode="promise_in_bounds")
            for a in range(8)
        ]
        p = {(a, b): columns[b][j + a:j + a + 1] for a in range(8) for b in range(a, 8)}
        inside = (local1 >= j) & (local1 < j + 8)
        rows = [
            jnp.where(inside, jnp.where(local1 == j + a, 1.0, 0.0), packed[j + a:j + a + 1])
            for a in range(8)
        ]
        change = jnp.zeros((32, 128), F32)
        for a in range(8):
            scale = 1.0 / p[a, a]
            for b in range(a + 1, 8):
                ratio = p[a, b] * scale
                for c in range(b, 8):
                    p[b, c] = p[b, c] - ratio * p[a, c]
                rows[b] = rows[b] - ratio * rows[a]
                columns[b] = columns[b] - columns[a] * ratio
            change = change + columns[a] * (rows[a] * scale)
            pivots[first + j + a:first + j + a + 1, :] = p[a, a]
        kept = jnp.where((local >= j) & (local < j + 8), 0.0, packed) - change
        packed = jnp.where(below, kept, packed)
        for a in range(8):
            packed = jnp.where(sub == j + a, rows[a], packed)
            roots = jnp.where(sub == j + a, lax.rsqrt(p[a, a]), roots)
        between()
        between()
    return jnp.where(local <= sub, packed, 0.0) * roots


def newton(a_ref, grad_ref, likelihood_ref, coef_ref, new_ref, objective_ref, pivots):
    lane = iota((1, 256), 1)
    for m in range(4):
        one_sided = a_ref[m]
        a_ref[m] = 0.5 * (one_sided + one_sided.T)
    blocks = [a_ref[m, 0:32, :] for m in range(4)]
    pending = []

    def between():
        if pending:
            pending.pop(0)()

    for k in range(8):
        low = 32 * k
        packed = jnp.concatenate([b[:, low:low + 32] for b in blocks], axis=1)
        inverse = factor_packed(packed, pivots, low, between)
        while pending:
            between()
        inside = (lane >= low) & (lane < low + 32)
        sign = jnp.where(lane < low, -1.0, 1.0)
        following = []
        for m in range(4):
            own = inverse[:, 32 * m:32 * m + 32]
            wide = jnp.concatenate(
                ([jnp.zeros((32, low), F32)] if low else []) + [own]
                + ([jnp.zeros((32, 224 - low), F32)] if low < 224 else []),
                axis=1,
            )
            half = jnp.where(inside, wide, dot6(own, blocks[m], (((1,), (0,)), ((), ()))))
            left = six_left(half * sign)
            right = six_right(half)
            skipped = [k]
            if k < 7:
                change = lax.dot_general(
                    left[:, low + 32:low + 64], right, TN, preferred_element_type=F32
                )
                ahead = jnp.where(inside, 0.0, a_ref[m, low + 32:low + 64, :]) - change
                following.append(ahead)
                a_ref[m, low + 32:low + 64, :] = ahead
                skipped.append(k + 1)

            def bulk(part, m=m, low=low, own=own, left=left, right=right, inside=inside,
                     skipped=skipped):
                change = lax.dot_general(
                    left[:, 128 * part:128 * part + 128], right, TN, preferred_element_type=F32
                )
                for n in range(4):
                    if 4 * part + n not in skipped:
                        rows = slice(128 * part + 32 * n, 128 * part + 32 * n + 32)
                        a_ref[m, rows, :] = (
                            jnp.where(inside, 0.0, a_ref[m, rows, :]) - change[32 * n:32 * n + 32]
                        )
                if part == 1:
                    a_ref[m, low:low + 32, :] = lax.dot_general(
                        six_left(own), right, TN, preferred_element_type=F32
                    )

            pending += [functools.partial(bulk, part) for part in range(2)]
        blocks = following
    while pending:
        between()
    logs = jnp.sum(jnp.log(pivots[...]), axis=0, keepdims=True)
    side_lane = iota((1, 128), 1)
    news = []
    for m in range(4):
        coef = coef_ref[m:m + 1, :]
        gradient = grad_ref[m] - LAMBDA * coef
        update = dot6(gradient, a_ref[m], (((1,), (0,)), ((), ())))
        new = coef + update[0:1]
        new_ref[m:m + 1, :] = new
        news += [new[:, :128], new[:, 128:]]
        half_logdet = 0.5 * jnp.sum(jnp.where(side_lane == 32 * m, logs, 0.0))
        likelihood = jnp.sum(jnp.where(side_lane == 0, likelihood_ref[m:m + 1, :], 0.0))
        objective_ref[m] = likelihood - 0.5 * LAMBDA * jnp.sum(coef * coef) - half_logdet
    return jnp.concatenate(news, axis=0)


def step_kernel(
    v_hbm, ids_hbm, w_hbm, member_hbm, label_hbm, z_hbm, slots_hbm, coef_hbm,
    new_ref, objective_ref, margin_ref,
    v_ref, ids_ref, w_ref, member_ref, label_ref, z_ref, slots_ref, coef_ref,
    onehot, ids2, part, fixed_part, fixed_recv, fixed_ref, table, wide, target_ref, slot_ref,
    send, recv, side_send, side_recv, a_ref, grad_ref, likelihood_ref, pivots,
    load_sem, table_sem, fixed_sem, side_sem, rows_send_sem, rows_recv_sem,
):
    torus = Torus()

    loads = [
        pltpu.make_async_copy(source, target, load_sem.at[n])
        for n, (source, target) in enumerate((
            (member_hbm, member_ref), (slots_hbm, slots_ref), (z_hbm, z_ref),
            (ids_hbm, ids_ref), (w_hbm, w_ref), (v_hbm, v_ref), (label_hbm, label_ref),
            (coef_hbm, coef_ref),
        ))
    ]
    for load in loads:
        load.start()

    barrier = pltpu.get_barrier_semaphore()
    greeted = iter(range(1, 128))

    def greet(count):
        for _ in range(count):
            k = next(greeted, None)
            if k is not None:
                pl.semaphore_signal(
                    barrier, inc=1, device_id=torus.peer(k), device_id_type=MESH
                )

    greet(127)
    loads[0].wait()
    loads[1].wait()
    for c in range(8):
        lanes = pl.ds(256 * c, 256)
        onehot[:, lanes] = one_hot(iota((512, 256), 0) == member_ref[:, lanes])
        greet(5)
    slots = slots_ref[...]
    sub = iota((8, 512), 0)
    owner = slots // 4
    owner_row = jnp.where(sub == 1, lax.rem(slots, 4), jnp.where(sub == 2, table_place(owner), 0))
    owner_row = jnp.where(sub == 0, torus.step_of(owner), owner_row).astype(F32).astype(BF16)
    before = one_hot(iota((256, 256), 0) < iota((256, 256), 1))
    tally = jnp.concatenate([before, jnp.ones((256, 256), BF16)], axis=1)
    base = jnp.zeros((512, 256), F32)
    for c in range(8):
        lanes = pl.ds(256 * c, 256)
        hot = onehot[:, lanes]
        found = jnp.dot(owner_row, hot, preferred_element_type=F32)
        counted = jnp.dot(hot, tally, preferred_element_type=F32)
        rank = jnp.sum(hot.astype(F32) * (base + counted[:, :256]), axis=0, keepdims=True)
        base = base + counted[:, 256:]
        slot_ref[:, lanes] = (found[2:3] * 4.0 + found[1:2]).astype(jnp.int32)
        target = found[0:1] * 32.0 + found[1:2] * 8.0 + rank
        target_ref[:, lanes] = target.astype(jnp.int32)
        greet(5)

    def pick_rows(c, carry):
        target = target_ref[...] - c * 256
        picked = jnp.zeros((256, 256), F32)
        for piece in range(4):
            lanes = pl.ds(512 * piece, 512)
            hot = one_hot(iota((256, 512), 0) == target[:, 512 * piece:512 * piece + 512])
            picked = picked + jnp.dot(hot, z_ref[lanes, :], preferred_element_type=F32)
        send[pl.ds(c * 8, 8)] = picked.astype(BF16).reshape(8, 32, 256)
        return carry

    def row_copy(places, k, phase):
        return remote(
            send.at[places], recv.at[places], rows_send_sem, rows_recv_sem.at[phase],
            torus.peer(k),
        )

    def pick(low, high):
        lax.fori_loop(low // 8, high // 8, pick_rows, 0)

    def send_rows(low, high, phase):
        for k in range(max(low, 1), high):
            row_copy(k, k, phase).start()

    def send_phase(phase):
        pick(PHASES[phase], PHASES[phase + 1])
        send_rows(PHASES[phase], PHASES[phase + 1], phase)

    for load in loads[3:]:
        load.wait()
    for r in range(64):
        for k in range(2):
            ids2[k, r:r + 1, :] = ids_ref[k:k + 1, 128 * r:128 * r + 128]
    spread = [one_hot(iota((128, 256), 1) == 2 * iota((128, 256), 0) + k) for k in range(2)]
    part[...] = sum(
        jnp.dot(ids2[k].astype(F32).astype(BF16), spread[k], preferred_element_type=F32)
        for k in range(2)
    )
    w2 = jnp.concatenate(halves(w_ref[...]), axis=1)

    def margin_rows(r, carry):
        rows = v_ref[pl.ds(pl.multiple_of(r * 256, 256), 256), :]
        product = lax.dot_general(
            w2, jnp.concatenate([rows, rows], axis=1), NT, preferred_element_type=F32
        )
        chosen = iota((128, 256), 0) == part[pl.ds(r, 1), :].astype(jnp.int32)
        part[pl.ds(r, 1), :] = jnp.sum(jnp.where(chosen, product, 0.0), axis=0, keepdims=True)
        return carry

    lax.fori_loop(0, 64, margin_rows, 0, unroll=8)
    pairs = one_hot(iota((256, 128), 0) // 2 == iota((256, 128), 1))
    fixed_part[...] = sum(
        jnp.dot(piece, pairs, preferred_element_type=F32) for piece in thirds(part[...])
    )

    loads[2].wait()
    pick(0, 8)
    pl.semaphore_wait(barrier, 127)
    for k in range(1, 4):
        remote(
            fixed_part.at[pl.ds(pl.multiple_of(torus.ys[k] * 16, 16), 16)],
            fixed_recv.at[pl.ds(k * 16, 16)],
            fixed_sem.at[0], fixed_sem.at[1],
            (lax.axis_index("dp"), torus.ys[k]),
        ).start()
    send_rows(0, 8, 0)
    pick(8, PHASES[1])
    send_rows(8, PHASES[1], 0)
    recv[0] = send[0]

    waiting = remote(
        fixed_part.at[pl.ds(0, 48)], fixed_recv.at[pl.ds(16, 48)],
        fixed_sem.at[0], fixed_sem.at[1], torus.peer(0),
    )
    waiting.wait_send()
    waiting.wait_recv()
    own = fixed_part[pl.ds(pl.multiple_of(torus.y * 16, 16), 16), :]
    total = own + fixed_recv[16:32] + fixed_recv[32:48] + fixed_recv[48:64]
    for r in range(16):
        fixed_ref[:, 128 * r:128 * r + 128] = total[r:r + 1, :]
    fixed = fixed_ref[...]
    code = label_ref[...].astype(F32) + 1.0
    target = target_ref[...]
    sides = jnp.zeros((128, 128), F32)
    for c in range(4):
        lanes = slice(512 * c, 512 * c + 512)
        step_hot = one_hot(iota((128, 512), 0) == target[:, lanes] // 32)
        within = iota((32, 512), 0) == lax.rem(target[:, lanes], 32)
        values = jnp.concatenate(
            [jnp.where(within, q[:, lanes], 0.0) for q in (fixed, code)]
            + [jnp.zeros((64, 512), F32)],
            axis=0,
        )
        for piece in thirds(values):
            sides = sides + lax.dot_general(step_hot, piece, NT, preferred_element_type=F32)
    for k in range(128):
        side_send[k] = sides[k:k + 1, :]

    def side_copy(places, k):
        return remote(
            side_send.at[places], side_recv.at[places], side_sem.at[0], side_sem.at[1],
            torus.peer(k),
        )

    for k in range(1, 128):
        side_copy(k, k).start()
    side_recv[0] = side_send[0]

    for phase in range(1, len(PHASES) - 1):
        send_phase(phase)

    waiting = side_copy(pl.ds(0, 127), 0)
    waiting.wait_send()
    waiting.wait_recv()
    eye = jnp.where(iota((256, 256), 0) == iota((256, 256), 1), LAMBDA, 0.0)
    ones = jnp.ones((256, 128), BF16)
    for phase in range(len(PHASES) - 1):
        low, high = PHASES[phase], PHASES[phase + 1]
        count = high - low
        row_copy(pl.ds(0, count - (phase == 0)), 0, phase).wait_recv()
        lane = iota((count, 8, 128), 2) - iota((count, 8, 128), 1)
        sides = jnp.broadcast_to(side_recv[low:high], (count, 8, 128))
        for m in range(4):
            rows = recv[low:high, 8 * m:8 * m + 8, :].astype(F32).reshape(8 * count, 256)
            rows_b = rows.astype(BF16)
            coef_b = jnp.broadcast_to(coef_ref[m:m + 1, :], (128, 256)).astype(BF16)
            known = jnp.where(lane == 8 * m, sides, 0.0).reshape(8 * count, 128)
            known = jnp.concatenate(halves(known), axis=1)
            score = lax.dot_general(rows_b, coef_b, NT, preferred_element_type=F32)
            score = score + jnp.dot(known, ones, preferred_element_type=F32)
            code = jnp.where(lane == 32 + 8 * m, sides, 0.0).reshape(8 * count, 128)
            code = jnp.dot(code.astype(BF16), ones[:128], preferred_element_type=F32)
            live = code > 0.5
            label = code - 1.0
            small = jnp.exp(-jnp.abs(score))
            inverse = 1.0 / (1.0 + small)
            probability = jnp.where(score >= 0.0, 1.0, small) * inverse
            weight = jnp.where(live, small * inverse * inverse, 0.0)
            residual = jnp.where(live, label - probability, 0.0).astype(BF16)
            gain = label * score - (jnp.maximum(score, 0.0) + jnp.log1p(small))
            gain = jnp.sum(jnp.where(live, gain, 0.0), axis=0, keepdims=True)
            weighted = (jnp.concatenate([weight, weight], axis=1) * rows).astype(BF16)
            update = lax.dot_general(weighted, rows_b, TN, preferred_element_type=F32)
            pull = lax.dot_general(residual, rows_b, TN, preferred_element_type=F32)[0:8]
            if phase == 0:
                a_ref[m] = eye + update
                grad_ref[m] = pull
                likelihood_ref[m:m + 1, :] = gain
            else:
                a_ref[m] += update
                grad_ref[m] += pull
                likelihood_ref[m:m + 1, :] += gain

    block = newton(a_ref, grad_ref, likelihood_ref, coef_ref, new_ref, objective_ref, pivots)
    row_copy(pl.ds(0, 127), 0, 0).wait_send()

    at = torus.table_place()
    table[pl.ds(at, 1)] = block.astype(BF16).reshape(1, 8, 128)

    def table_copy(blocks, number, peer):
        return remote(
            table.at[blocks], table.at[blocks], table_sem.at[number], table_sem.at[2 + number],
            peer,
        )

    for k in range(1, 64):
        table_copy(pl.ds(at, 1), 0, torus.chip_peer(k)).start()
    waiting = table_copy(pl.ds(0, 63), 0, torus.sibling())
    waiting.wait_send()
    waiting.wait_recv()
    swap = table_copy(pl.ds(torus.core * 64, 64), 1, torus.sibling())
    swap.start()
    margin_ref[...] = fixed_ref[...]

    def add_margins(core):
        here = pl.ds(core * 64, 64)
        rows = pl.ds(pl.multiple_of(core * 512, 512), 512)
        wide[rows, :] = table[here].astype(F32).reshape(512, 128)
        add_row_products(wide, core * 256, z_ref, slot_ref, margin_ref)

    add_margins(torus.core)
    swap.wait_send()
    swap.wait_recv()
    add_margins(torus.cores[1])


def step(v, ids, fixed_coef, member, labels, z, slots, coef):
    vmem = pl.BlockSpec(memory_space=pltpu.VMEM)
    operands = (v, ids, fixed_coef, member, labels, z, slots, coef)
    return pl.pallas_call(
        step_kernel,
        out_shape=(
            jax.ShapeDtypeStruct((4, 256), F32),
            jax.ShapeDtypeStruct((4,), F32),
            jax.ShapeDtypeStruct((1, 2048), F32),
        ),
        in_specs=[pl.BlockSpec(memory_space=pl.ANY)] * 8,
        out_specs=(vmem, pl.BlockSpec(memory_space=pltpu.SMEM), vmem),
        scratch_shapes=[pltpu.VMEM(x.shape, x.dtype) for x in operands] + [
            pltpu.VMEM((512, 2048), BF16),
            pltpu.VMEM((2, 64, 128), jnp.int32),
            pltpu.VMEM((64, 256), F32),
            pltpu.VMEM((64, 128), F32),
            pltpu.VMEM((64, 128), F32),
            pltpu.VMEM((1, 2048), F32),
            pltpu.VMEM((128, 8, 128), BF16),
            pltpu.VMEM((1024, 128), F32),
            pltpu.VMEM((1, 2048), jnp.int32),
            pltpu.VMEM((1, 2048), jnp.int32),
            pltpu.VMEM((128, 32, 256), BF16),
            pltpu.VMEM((128, 32, 256), BF16),
            pltpu.VMEM((128, 1, 128), F32),
            pltpu.VMEM((128, 1, 128), F32),
            pltpu.VMEM((4, 256, 256), F32),
            pltpu.VMEM((4, 8, 256), F32),
            pltpu.VMEM((4, 128), F32),
            pltpu.VMEM((256, 128), F32),
            pltpu.SemaphoreType.DMA((8,)),
            pltpu.SemaphoreType.DMA((4,)),
            pltpu.SemaphoreType.DMA((2,)),
            pltpu.SemaphoreType.DMA((2,)),
            pltpu.SemaphoreType.DMA,
            pltpu.SemaphoreType.DMA((len(PHASES) - 1,)),
        ],
        compiler_params=pltpu.CompilerParams(
            collective_id=0, has_side_effects=True, vmem_limit_bytes=56 * MIB
        ),
        name="step",
    )(*operands)


def hand_over_kernel(*refs):
    count = (len(refs) - 1) // 2
    copies = [
        pltpu.make_async_copy(refs[n], refs[count + n], refs[-1].at[n]) for n in range(count)
    ]
    for copy in copies:
        copy.start()
    for copy in copies:
        copy.wait()


def hand_over(*arrays):
    anywhere = pl.BlockSpec(memory_space=pl.ANY)
    return pl.pallas_call(
        hand_over_kernel,
        out_shape=tuple(jax.ShapeDtypeStruct(x.shape, x.dtype) for x in arrays),
        in_specs=[anywhere] * len(arrays),
        out_specs=(anywhere,) * len(arrays),
        scratch_shapes=[pltpu.SemaphoreType.DMA((len(arrays),))],
        name="hand_over",
    )(*arrays)


def shards(feat_values, feat_blocks, fixed_coef, member_of, labels, re_features, member_slot, coef):
    new_coef, objective, margin = step(
        feat_values.reshape(16384, 128),
        feat_blocks.T,
        fixed_coef,
        member_of.reshape(1, 2048),
        labels.reshape(1, 2048),
        re_features,
        member_slot.reshape(1, 512),
        coef,
    )
    new_coef, objective, margin = hand_over(new_coef, objective, margin)
    return (new_coef, objective, margin.reshape(2048))


def solution(mesh):
    placed = (
        P("dp", "mp", None),
        P("dp", "mp"),
        P(),
        P(("dp", "mp"), None),
        P(("dp", "mp")),
        P(("dp", "mp"), None),
        P(),
        P(("dp", "mp"), None),
    )
    return jax.shard_map(
        shards,
        mesh=mesh,
        in_specs=placed,
        out_specs=(P(("dp", "mp"), None), P(("dp", "mp")), P(("dp", "mp"))),
        check_vma=False,
    )
```
